128 devices in a mesh: gx: 32 (over y, z, x_lo), gy: 4 (over x_hi, core).
Axes of the slice: x: 4 (x_hi: 2, x_lo: 2; x = x_hi * 2 + x_lo), y: 4, z: 4, core: 2. Of those that a mesh axis runs over, the one named last changes fastest.
Arguments:
- right_side: float32 [2, 2048, 256, 128], P(None, 'gx', 'gy'), may hold values from -8 to 8
- well_coef: float32 [2048, 256, 128], P('gx', 'gy'), may hold values from 2 to 6
- mobility_coef: float32 [2048, 256, 128], P('gx', 'gy'), may hold values from 2 to 6
- coupling: float32 [2048, 256, 128], P('gx', 'gy'), may hold values from -0.5 to 0.5
- phase_old: float32 [2048, 256, 128], P('gx', 'gy'), may hold values from -1 to 1
- unit_owner: int32 [16384], P(('gx', 'gy')), may hold values from 0 to 127, as said below
- velocity: float32 [3, 16384, 512], P(None, ('gx', 'gy')), may hold values from -4 to 4
Outputs:
- correction: float32 [2, 2048, 256, 128], P(None, 'gx', 'gy')
- momentum: float32 [3, 16384, 512], P(None, ('gx', 'gy'))
The draws below stay inside these ranges and needn't reach their ends.
Inputs may be any that keep to these rules, and one draw needn't show every extreme that they name: `unit_owner`: each device's 128 units go to 128 different owners, and every owner receives exactly one unit from each device.
All inputs are finite; a program needn't handle non-finite values.
Results may differ from the reference program's by a relative error of at most 0.000088.
Values sent between devices are 32-bit elements; how exact they have to be, the bound alone decides.
A program may use at most 128 MiB of HBM per device.

```python
import math
import jax
import jax.numpy as jnp

CX = 64
CY = 64
CZ = 128
SWEEPS = 3
NX = 2048
NY = 256
NZ = 128
UNITS_DEV = 128
UNITS = 16384
UNIT_NODES = 512


def draw_unit_owner(key, part):
    first, second, third = jax.random.split(jax.random.fold_in(key, 7), 3)
    count = UNITS_DEV
    row_perm = jax.random.permutation(first, count)
    col_perm = jax.random.permutation(second, count)
    label = jax.random.permutation(third, count)
    square = (row_perm[:, None] + col_perm[None, :]) % count
    return label[square].reshape(-1).astype(jnp.int32)


def steps_of(rng, shape, cuts, smallest, top_value):
    gain, own = 1.0, jax.random.fold_in(rng, 6)
    for dim, shards_of in cuts:
        steps = jnp.exp(jax.random.uniform(jax.random.fold_in(own, dim), (shards_of,), jnp.float32, smallest / len(cuts), top_value / len(cuts)))
        gain = gain * jnp.repeat(steps, shape[dim] // shards_of).reshape([-1 if axis == dim else 1 for axis in range(len(shape))])
    return gain


def bell_draw(key, extent, scale, bound, cuts=(), kind=jnp.bfloat16):
    values = jax.random.normal(key, extent, jnp.float32) * scale
    if len(cuts) > 0:
        values = steps_of(key, extent, cuts, -0.22, 0.18) * values
    return jnp.clip(values, min=-bound, max=bound).astype(kind)


def setup_inputs(seed: int = 0) -> dict:
    splits = jax.random.split(jax.random.key(seed), 8)
    return {
        "right_side": bell_draw(splits[0], (2, NX, NY, NZ), 1.0, 8.0, ((1, 32), (2, 4)), jnp.float32),
        "well_coef": jnp.clip(jnp.exp(math.log(6.0) - 1.0986123 * jax.random.uniform(splits[1], (NX, NY, NZ), jnp.float32) ** steps_of(splits[1], (NX, NY, NZ), ((0, 32), (1, 4)), -0.2, 0.2)), 2.0, 6.0),
        "mobility_coef": jnp.clip(jnp.exp(math.log(6.0) - 1.0986123 * jax.random.uniform(splits[2], (NX, NY, NZ), jnp.float32) ** steps_of(splits[2], (NX, NY, NZ), ((0, 32), (1, 4)), -0.2, 0.2)), 2.0, 6.0),
        "coupling": jnp.clip(jax.random.uniform(splits[3], (NX, NY, NZ), jnp.float32, -0.5, 0.5) * steps_of(splits[3], (NX, NY, NZ), ((0, 32), (1, 4)), -0.4, 0.0), -0.5, 0.5),
        "phase_old": jnp.clip(jax.random.uniform(splits[4], (NX, NY, NZ), jnp.float32, -1.0, 1.0) * steps_of(splits[4], (NX, NY, NZ), ((0, 32), (1, 4)), -0.4, 0.0), -1.0, 1.0),
        "unit_owner": draw_unit_owner(jax.random.fold_in(splits[7], 71), 0),
        "velocity": bell_draw(splits[6], (3, UNITS, UNIT_NODES), 0.3, 4.0, ((1, 128),), jnp.float32),
    }


LOW_BOUND = 0.15
HIGH_BOUND = 1.85


def block_apply(center, padded_xy, well_coef, mobility_coef, coupling):
    full = jnp.pad(padded_xy, ((0, 0), (0, 0), (0, 0), (1, 1)))
    beside = full[:, 2:, 1:-1, 1:-1] + full[:, :-2, 1:-1, 1:-1]
    beside = beside + full[:, 1:-1, 2:, 1:-1] + full[:, 1:-1, :-2, 1:-1]
    beside = beside + full[:, 1:-1, 1:-1, 2:] + full[:, 1:-1, 1:-1, :-2]
    lapl = 6.0 * center - beside
    first = well_coef * center[0] + lapl[0] + coupling * center[1]
    second = coupling * center[0] + mobility_coef * center[1] + lapl[1]
    return jnp.stack([first, second])


def chebyshev(right_side, well_coef, mobility_coef, coupling, faces):
    theta = (HIGH_BOUND + LOW_BOUND) / 2.0
    delta = (HIGH_BOUND - LOW_BOUND) / 2.0
    sigma = theta / delta
    inv_diag = jnp.stack([1.0 / (well_coef + 6.0), 1.0 / (mobility_coef + 6.0)])
    resid = right_side
    rho_now = 1.0 / sigma
    direc = inv_diag * resid * (1.0 / theta)
    total = direc
    for sweep in range(SWEEPS):
        resid = resid - block_apply(direc, faces(direc), well_coef, mobility_coef, coupling)
        rho_new = 1.0 / (2.0 * sigma - rho_now)
        direc = (rho_new * rho_now) * direc + (2.0 * rho_new / delta) * (inv_diag * resid)
        total = total + direc
        rho_now = rho_new
    return total


def fields_of(phase, padded_phase, chem):
    full = jnp.pad(padded_phase, ((0, 0), (0, 0), (1, 1)))
    grad_x = (full[2:, 1:-1, 1:-1] - full[:-2, 1:-1, 1:-1]) * 0.5
    grad_y = (full[1:-1, 2:, 1:-1] - full[1:-1, :-2, 1:-1]) * 0.5
    grad_z = (full[1:-1, 1:-1, 2:] - full[1:-1, 1:-1, :-2]) * 0.5
    density = 0.1 + 0.9 * (1.0 + phase) * 0.5
    viscosity = 0.2 + 0.8 * (1.0 + phase) * 0.5
    return jnp.stack([density, viscosity, chem * grad_x, chem * grad_y, chem * grad_z])


def restrict(fields):
    comps, sx, sy, sz = fields.shape
    blocks = fields.reshape(comps, sx // 2, 2, sy // 2, 2, sz // 2, 2)
    return jnp.mean(blocks, axis=(2, 4, 6))


def column_operator(vel, density, viscosity, length):
    shape = vel.shape
    vcol = vel.reshape(shape[0], shape[1], shape[2] // length, length)
    dcol = density.reshape(1, shape[1], shape[2] // length, length)
    ecol = viscosity.reshape(1, shape[1], shape[2] // length, length)
    efac = 0.5 * (ecol[..., 1:] + ecol[..., :-1])
    inner = efac * (vcol[..., 1:] - vcol[..., :-1])
    flux = jnp.concatenate([ecol[..., :1] * vcol[..., :1], inner, -ecol[..., -1:] * vcol[..., -1:]], axis=-1)
    out = dcol * vcol - (flux[..., 1:] - flux[..., :-1])
    return out.reshape(shape)


def momentum_of(recv, vel, length):
    density = recv[0]
    viscosity = recv[1]
    force = recv[2:5]
    stress = column_operator(vel, density, viscosity, length) - force
    return column_operator(stress, density, viscosity, length)


def reference(right_side, well_coef, mobility_coef, coupling, phase_old, unit_owner, velocity):
    def faces(field):
        return jnp.pad(field, ((0, 0), (1, 1), (1, 1), (0, 0)))

    correction = chebyshev(right_side, well_coef, mobility_coef, coupling, faces)
    phase = phase_old + correction[0]
    padded_phase = jnp.pad(phase, ((1, 1), (1, 1), (0, 0)))
    coarse = restrict(fields_of(phase, padded_phase, correction[1]))
    ngx = NX // CX
    ngy = NY // CY
    ndev = ngx * ngy
    blocks = coarse.reshape(5, ngx, CX // 2, ngy, CY // 2, CZ // 2)
    blocks = jnp.transpose(blocks, (0, 1, 3, 2, 4, 5)).reshape(5, ndev * ndev, UNIT_NODES)
    source = jnp.repeat(jnp.arange(ndev, dtype=jnp.int32), ndev)
    rows = (unit_owner.astype(jnp.int32) * ndev + source).astype(jnp.int32)
    vel_src = velocity[:, rows, :]
    result = momentum_of(blocks, vel_src, CZ // 2)
    momentum = jnp.zeros((3, ndev * ndev, UNIT_NODES), jnp.float32).at[:, rows, :].set(result)
    return correction, momentum
```

```python
import functools

import jax
import jax.numpy as jnp
from jax import lax
from jax.experimental import pallas as pl
from jax.experimental.pallas import tpu as pltpu
from jax.sharding import PartitionSpec as P

SWEEPS = 3
LOW_BOUND = 0.15
HIGH_BOUND = 1.85
THETA = (HIGH_BOUND + LOW_BOUND) / 2.0
DELTA = (HIGH_BOUND - LOW_BOUND) / 2.0
SIGMA = THETA / DELTA

PAD = 8
MESH = pl.DeviceIdType.MESH


def recurrence():
    out = []
    rho = 1.0 / SIGMA
    decay_before, gain_before = 0.0, 0.0
    for sweep in range(SWEEPS):
        rho_new = 1.0 / (2.0 * SIGMA - rho)
        decay, gain = rho_new * rho, 2.0 * rho_new / DELTA
        if sweep == 0:
            out.append((decay + gain * (THETA - 1.0), 0.0, gain))
        else:
            ratio = gain / gain_before
            out.append((decay + ratio - gain, -ratio * decay_before, gain))
        decay_before, gain_before, rho = decay, gain, rho_new
    return out


def kernel_body(
    sizes,
    order,
    rhs_hbm,
    well_hbm,
    mob_hbm,
    cpl_hbm,
    pold_hbm,
    vel_hbm,
    corr_hbm,
    mom_hbm,
    rhs,
    inv,
    cpl,
    pold,
    dir0,
    dir1,
    dir2,
    phase,
    slab,
    packed,
    stage,
    recv,
    vel,
    mom,
    load_sem,
    rest_sem,
    out_sem,
    halo_send,
    halo_recv,
    unit_send,
    unit_recv,
):
    ngx, ngy, cx, cy, cz, chunks = sizes
    ndev = ngx * ngy
    gx, gy = lax.axis_index("gx"), lax.axis_index("gy")
    me = gx * ngy + gy
    per = cx // chunks
    lo, hi = PAD, PAD + cy
    unit_rows = packed.shape[1]

    def load_chunk(i):
        at = pl.ds(i * per, per)
        return (
            pltpu.make_async_copy(rhs_hbm.at[:, at], rhs.at[:, at], load_sem.at[i, 0]),
            pltpu.make_async_copy(well_hbm.at[at], inv.at[0, at], load_sem.at[i, 1]),
            pltpu.make_async_copy(mob_hbm.at[at], inv.at[1, at], load_sem.at[i, 2]),
        )

    load_cpl = pltpu.make_async_copy(cpl_hbm, cpl, rest_sem.at[0])
    load_pold = pltpu.make_async_copy(pold_hbm, pold, rest_sem.at[1])
    load_vel = pltpu.make_async_copy(vel_hbm, vel, rest_sem.at[2])
    chunk_order = [0, chunks - 1] + list(range(1, chunks - 1))
    for i in chunk_order:
        for copy in load_chunk(i):
            copy.start()
    load_cpl.start()
    load_pold.start()
    load_vel.start()

    for buf in (dir0, dir1, dir2):
        @pl.when(gx == 0)
        def _(buf=buf):
            buf[:, 0, lo:hi, :] = jnp.zeros((2, cy, cz), jnp.float32)

        @pl.when(gx == ngx - 1)
        def _(buf=buf):
            buf[:, cx + 1, lo:hi, :] = jnp.zeros((2, cy, cz), jnp.float32)

        @pl.when(gy == 0)
        def _(buf=buf):
            buf[:, 1 : cx + 1, lo - 1 : lo, :] = jnp.zeros((2, cx, 1, cz), jnp.float32)

        @pl.when(gy == ngy - 1)
        def _(buf=buf):
            buf[:, 1 : cx + 1, hi : hi + 1, :] = jnp.zeros((2, cx, 1, cz), jnp.float32)

    @pl.when(gx == 0)
    def _():
        phase[0, lo:hi, :] = jnp.zeros((cy, cz), jnp.float32)

    @pl.when(gx == ngx - 1)
    def _():
        phase[cx + 1, lo:hi, :] = jnp.zeros((cy, cz), jnp.float32)

    @pl.when(gy == 0)
    def _():
        phase[1 : cx + 1, lo - 1 : lo, :] = jnp.zeros((cx, 1, cz), jnp.float32)

    @pl.when(gy == ngy - 1)
    def _():
        phase[1 : cx + 1, hi : hi + 1, :] = jnp.zeros((cx, 1, cz), jnp.float32)

    def halo_copy(step, ref, way):
        lead = (slice(None),) if len(ref.shape) == 4 else ()
        own, rows = slice(lo, hi), slice(1, cx + 1)
        src, dst, target = (
            ((1, own), (cx + 1, own), (gx - 1, gy)),
            ((cx, own), (0, own), (gx + 1, gy)),
            ((rows, slice(lo, lo + 1)), (rows, slice(hi, hi + 1)), (gx, gy - 1)),
            ((rows, slice(hi - 1, hi)), (rows, slice(lo - 1, lo)), (gx, gy + 1)),
        )[way]
        return pltpu.make_async_remote_copy(
            src_ref=ref.at[lead + src],
            dst_ref=ref.at[lead + dst],
            send_sem=halo_send.at[step, way],
            recv_sem=halo_recv.at[step, way],
            device_id=target,
            device_id_type=MESH,
        )

    sends = (gx > 0, gx < ngx - 1, gy > 0, gy < ngy - 1)
    receives = (gx < ngx - 1, gx > 0, gy < ngy - 1, gy > 0)

    def send(step, ref, ways):
        for way in ways:

            @pl.when(sends[way])
            def _(way=way):
                halo_copy(step, ref, way).start()

    def receive(step, ref):
        for way in range(4):

            @pl.when(receives[way])
            def _(way=way):
                halo_copy(step, ref, way).wait_recv()

    def finish(step, ref):
        for way in range(4):

            @pl.when(sends[way])
            def _(way=way):
                halo_copy(step, ref, way).wait_send()

    lane = lax.broadcasted_iota(jnp.int32, (1, cz), 1)
    first_lane, last_lane = lane == 0, lane == cz - 1

    def along_depth(v):
        before = jnp.where(first_lane, 0.0, pltpu.roll(v, 1, axis=1))
        after = jnp.where(last_lane, 0.0, pltpu.roll(v, cz - 1, axis=1))
        return before, after

    def start_plane(x):
        for c in range(2):
            part = 1.0 / (inv[c, x] + 6.0)
            inv[c, x] = part
            dir0[c, x + 1, lo:hi, :] = part * rhs[c, x] * (1.0 / THETA)

    for n, i in enumerate(chunk_order):
        for copy in load_chunk(i):
            copy.wait()
        lax.fori_loop(i * per, (i + 1) * per, lambda x, _: (start_plane(x), 0)[1], 0)
        if n == 1:
            send(0, dir0, (0, 1))
    send(0, dir0, (2, 3))
    load_cpl.wait()

    table = recurrence()

    def sweep_rows(sweep, x, y, rows):
        now = (dir0, dir1, dir2)[sweep]
        of_now, of_before, of_update = table[sweep]
        at = pl.ds(lo + y, rows)
        mid = [now[c, x + 1, at, :] for c in range(2)]
        mix = cpl[x, pl.ds(y, rows), :]
        out = []
        for c in range(2):
            before, after = along_depth(mid[c])
            nbrs = now[c, x, at, :] + now[c, x + 2, at, :]
            nbrs = nbrs + now[c, x + 1, pl.ds(lo + y - 1, rows), :]
            nbrs = nbrs + now[c, x + 1, pl.ds(lo + y + 1, rows), :]
            nbrs = nbrs + (before + after)
            update = inv[c, x, pl.ds(y, rows), :] * (nbrs - mix * mid[1 - c])
            new = of_now * mid[c] + of_update * update
            if sweep > 0:
                new = new + of_before * (dir0, dir1)[sweep - 1][c, x + 1, at, :]
            out.append(new)
        if sweep < SWEEPS - 1:
            for c in range(2):
                (dir1, dir2)[sweep][c, x + 1, at, :] = out[c]
        else:
            for c in range(2):
                total = dir0[c, x + 1, at, :] + dir1[c, x + 1, at, :]
                total = total + mid[c] + out[c]
                rhs[c, x, pl.ds(y, rows), :] = total
                if c == 0:
                    phase[x + 1, at, :] = pold[x, pl.ds(y, rows), :] + total

    for sweep in range(SWEEPS):
        now = (dir0, dir1, dir2)[sweep]
        new = (dir1, dir2, phase)[sweep]
        receive(sweep, now)
        if sweep == SWEEPS - 1:
            load_pold.wait()
        sweep_rows(sweep, 0, 0, cy)
        sweep_rows(sweep, cx - 1, 0, cy)
        send(sweep + 1, new, (0, 1))

        def edges(x, _, sweep=sweep):
            sweep_rows(sweep, x, 0, 8)
            sweep_rows(sweep, x, cy - 8, 8)
            return 0

        lax.fori_loop(1, cx - 1, edges, 0)
        send(sweep + 1, new, (2, 3))

        def inner(x, _, sweep=sweep):
            sweep_rows(sweep, x, 8, cy - 16)
            return 0

        lax.fori_loop(1, cx - 1, inner, 0)

    store_corr = pltpu.make_async_copy(rhs, corr_hbm, out_sem.at[0])
    store_corr.start()
    receive(SWEEPS, phase)

    deep = lax.broadcasted_iota(jnp.int32, (2 * cz, cz), 0) // 2
    wide = lax.broadcasted_iota(jnp.int32, (2 * cz, cz), 1)
    pairing = jnp.where(deep == wide, 0.125, 0.0).astype(jnp.float32)

    def coarse_plane(i, _):
        sums = [None] * 4
        for x in (2 * i, 2 * i + 1):
            at = pl.ds(lo, cy)
            mid = phase[x + 1, at, :]
            half = 0.5 * rhs[1, x]
            before, after = along_depth(mid)
            fields = (
                mid,
                half * (phase[x + 2, at, :] - phase[x, at, :]),
                half * (phase[x + 1, pl.ds(lo + 1, cy), :] - phase[x + 1, pl.ds(lo - 1, cy), :]),
                half * (after - before),
            )
            sums = [f if s is None else s + f for s, f in zip(sums, fields)]
        for f in range(4):
            slab[f] = sums[f]
        rows = []
        quarter = cy // 4
        for f in range(4):
            part = [slab[f, pl.ds(k, quarter, stride=4), :] for k in range(4)]
            rows.append(jnp.concatenate([part[0] + part[1], part[2] + part[3]], axis=1))
        both = jnp.concatenate(rows, axis=0)
        mean = jnp.dot(
            both, pairing, precision=lax.Precision.HIGHEST, preferred_element_type=jnp.float32
        )
        for f in range(4):
            for q in range(4):
                base = f * quarter + q * 4
                packed[i * 4 + q, f * 4 : f * 4 + 4, :] = mean[base : base + 4, :]
        return 0

    lax.fori_loop(0, cx // 2, coarse_plane, 0)

    def unit_copy(peer):
        return pltpu.make_async_remote_copy(
            src_ref=stage.at[peer],
            dst_ref=recv.at[pl.ds(me * unit_rows, unit_rows)],
            send_sem=unit_send,
            recv_sem=unit_recv,
            device_id=(peer // ngy, peer % ngy),
            device_id_type=MESH,
        )

    def ship(k, _):
        peer = lax.rem(me + k, ndev)
        stage[peer] = packed[order[peer]]
        unit_copy(peer).start()
        return 0

    lax.fori_loop(1, ndev, ship, 0)
    recv[pl.ds(me * unit_rows, unit_rows), :] = packed[order[me]]

    for step, ref in enumerate((dir0, dir1, dir2, phase)):
        finish(step, ref)
    load_vel.wait()
    others = pl.ds(0, (ndev - 1) * unit_rows)
    pltpu.make_async_copy(recv.at[others], recv.at[others], unit_recv).wait()

    place = lax.rem(lane, cz // 2)
    bottom, top = place == 0, place == cz // 2 - 1

    def product(v, density, visc, weight):
        below = jnp.where(bottom, 0.0, pltpu.roll(v, 1, axis=1))
        flux = weight * (v - below)
        above = jnp.where(top, -visc * v, pltpu.roll(flux, cz - 1, axis=1))
        return density * v - (above - flux)

    for r in range(4):
        get = lambda f: recv[pl.ds(f * 4 + r, ndev, stride=unit_rows), :]
        mean = get(0)
        density = 0.1 + 0.45 * (1.0 + mean)
        visc = 0.2 + 0.4 * (1.0 + mean)
        weight = 0.5 * (visc + jnp.where(bottom, visc, pltpu.roll(visc, 1, axis=1)))
        for c in range(3):
            at = pl.ds(r * cz, cz)
            stress = product(vel[c, :, at], density, visc, weight) - get(c + 1)
            mom[c, :, at] = product(stress, density, visc, weight)

    store_mom = pltpu.make_async_copy(mom, mom_hbm, out_sem.at[1])
    store_mom.start()
    sent = pl.ds(0, ndev - 1)
    pltpu.make_async_copy(stage.at[sent], stage.at[sent], unit_send).wait()
    store_corr.wait()
    store_mom.wait()


def body(ngx, ngy, right_side, well_coef, mobility_coef, coupling, phase_old, unit_owner, velocity):
    _, cx, cy, cz = right_side.shape
    ndev = ngx * ngy
    chunks = 8
    unit_rows = 4 * (velocity.shape[2] // cz)
    ids = jnp.arange(ndev, dtype=jnp.int32)
    order = jnp.sum(jnp.where(unit_owner[None, :] == ids[:, None], ids[None, :], 0), axis=1)
    any_spec = pl.BlockSpec(memory_space=pl.ANY)
    padded = (cx + 2, cy + 2 * PAD, cz)
    f32 = jnp.float32
    return pl.pallas_call(
        functools.partial(kernel_body, (ngx, ngy, cx, cy, cz, chunks)),
        out_shape=(
            jax.ShapeDtypeStruct(right_side.shape, f32),
            jax.ShapeDtypeStruct(velocity.shape, f32),
        ),
        in_specs=[pl.BlockSpec(memory_space=pltpu.SMEM)] + [any_spec] * 6,
        out_specs=(any_spec, any_spec),
        scratch_shapes=[
            pltpu.VMEM((2, cx, cy, cz), f32),
            pltpu.VMEM((2, cx, cy, cz), f32),
            pltpu.VMEM((cx, cy, cz), f32),
            pltpu.VMEM((cx, cy, cz), f32),
            pltpu.VMEM((2,) + padded, f32),
            pltpu.VMEM((2,) + padded, f32),
            pltpu.VMEM((2,) + padded, f32),
            pltpu.VMEM(padded, f32),
            pltpu.VMEM((4, cy, cz), f32),
            pltpu.VMEM((ndev, unit_rows, cz), f32),
            pltpu.VMEM((ndev, unit_rows, cz), f32),
            pltpu.VMEM((ndev * unit_rows, cz), f32),
            pltpu.VMEM(velocity.shape, f32),
            pltpu.VMEM(velocity.shape, f32),
            pltpu.SemaphoreType.DMA((chunks, 3)),
            pltpu.SemaphoreType.DMA((3,)),
            pltpu.SemaphoreType.DMA((2,)),
            pltpu.SemaphoreType.DMA((SWEEPS + 1, 4)),
            pltpu.SemaphoreType.DMA((SWEEPS + 1, 4)),
            pltpu.SemaphoreType.DMA,
            pltpu.SemaphoreType.DMA,
        ],
        compiler_params=pltpu.CompilerParams(
            has_side_effects=True, vmem_limit_bytes=56 * 1024 * 1024
        ),
    )(order, right_side, well_coef, mobility_coef, coupling, phase_old, velocity)


def solution(mesh):
    return jax.shard_map(
        functools.partial(body, mesh.shape["gx"], mesh.shape["gy"]),
        mesh=mesh,
        in_specs=(
            P(None, "gx", "gy", None),
            P("gx", "gy", None),
            P("gx", "gy", None),
            P("gx", "gy", None),
            P("gx", "gy", None),
            P(("gx", "gy")),
            P(None, ("gx", "gy"), None),
        ),
        out_specs=(P(None, "gx", "gy", None), P(None, ("gx", "gy"), None)),
        check_vma=False,
    )
```

```python
import functools

import jax
import jax.numpy as jnp
from jax import lax
from jax.experimental import pallas as pl
from jax.experimental.pallas import tpu as pltpu
from jax.sharding import PartitionSpec as P

SWEEPS = 3
LOW_BOUND = 0.15
HIGH_BOUND = 1.85
THETA = (HIGH_BOUND + LOW_BOUND) / 2.0
DELTA = (HIGH_BOUND - LOW_BOUND) / 2.0
SIGMA = THETA / DELTA

PAD = 8
MESH = pl.DeviceIdType.MESH


def recurrence():
    table, scales = [], [1.0]
    rho = 1.0 / SIGMA
    decay_before, gain_before = 0.0, 0.0
    for sweep in range(SWEEPS):
        rho_new = 1.0 / (2.0 * SIGMA - rho)
        decay, gain = rho_new * rho, 2.0 * rho_new / DELTA
        if sweep == 0:
            table.append(((decay + gain * (THETA - 1.0)) / gain, 0.0))
        else:
            ratio = gain / gain_before
            before = -ratio * decay_before * scales[-2] / (gain * scales[-1])
            table.append(((decay + ratio - gain) / gain, before))
        scales.append(scales[-1] * gain)
        decay_before, gain_before, rho = decay, gain, rho_new
    return table, scales


def kernel_body(
    sizes,
    order,
    rhs_hbm,
    well_hbm,
    mob_hbm,
    cpl_hbm,
    pold_hbm,
    vel_hbm,
    corr_hbm,
    mom_hbm,
    rhs,
    inv,
    cpl,
    pold,
    dir0,
    dir1,
    dir2,
    phase,
    slab,
    packed,
    stage,
    recv,
    vel,
    mom,
    load_sem,
    rest_sem,
    out_sem,
    halo_send,
    halo_recv,
    unit_send,
    unit_recv,
):
    ngx, ngy, cx, cy, cz, chunks = sizes
    ndev = ngx * ngy
    gx, gy = lax.axis_index("gx"), lax.axis_index("gy")
    me = gx * ngy + gy
    per = cx // chunks
    lo, hi = PAD, PAD + cy
    unit_rows = packed.shape[1]

    def load_chunk(i):
        at = pl.ds(i * per, per)
        return (
            pltpu.make_async_copy(rhs_hbm.at[:, at], rhs.at[:, at], load_sem.at[i, 0]),
            pltpu.make_async_copy(well_hbm.at[at], inv.at[0, at], load_sem.at[i, 1]),
            pltpu.make_async_copy(mob_hbm.at[at], inv.at[1, at], load_sem.at[i, 2]),
        )

    load_cpl = pltpu.make_async_copy(cpl_hbm, cpl, rest_sem.at[0])
    load_pold = pltpu.make_async_copy(pold_hbm, pold, rest_sem.at[1])
    load_vel = pltpu.make_async_copy(vel_hbm, vel, rest_sem.at[2])
    chunk_order = [0, chunks - 1] + list(range(1, chunks - 1))
    for i in chunk_order:
        for copy in load_chunk(i):
            copy.start()
    load_cpl.start()
    load_pold.start()
    load_vel.start()

    barrier = pltpu.get_barrier_semaphore()

    def greet(k, _):
        peer = lax.rem(me + k, ndev)
        pl.semaphore_signal(
            barrier, inc=1, device_id=(peer // ngy, lax.rem(peer, ngy)), device_id_type=MESH
        )
        return 0

    lax.fori_loop(1, ndev, greet, 0)

    for buf in (dir0, dir1, dir2):
        @pl.when(gx == 0)
        def _(buf=buf):
            buf[:, 0, lo:hi, :] = jnp.zeros((2, cy, cz), jnp.float32)

        @pl.when(gx == ngx - 1)
        def _(buf=buf):
            buf[:, cx + 1, lo:hi, :] = jnp.zeros((2, cy, cz), jnp.float32)

        @pl.when(gy == 0)
        def _(buf=buf):
            buf[:, 1 : cx + 1, lo - 1 : lo, :] = jnp.zeros((2, cx, 1, cz), jnp.float32)

        @pl.when(gy == ngy - 1)
        def _(buf=buf):
            buf[:, 1 : cx + 1, hi : hi + 1, :] = jnp.zeros((2, cx, 1, cz), jnp.float32)

    @pl.when(gx == 0)
    def _():
        phase[0, lo:hi, :] = jnp.zeros((cy, cz), jnp.float32)

    @pl.when(gx == ngx - 1)
    def _():
        phase[cx + 1, lo:hi, :] = jnp.zeros((cy, cz), jnp.float32)

    @pl.when(gy == 0)
    def _():
        phase[1 : cx + 1, lo - 1 : lo, :] = jnp.zeros((cx, 1, cz), jnp.float32)

    @pl.when(gy == ngy - 1)
    def _():
        phase[1 : cx + 1, hi : hi + 1, :] = jnp.zeros((cx, 1, cz), jnp.float32)

    def halo_copy(step, ref, way):
        lead = (slice(None),) if len(ref.shape) == 4 else ()
        own, rows = slice(lo, hi), slice(1, cx + 1)
        src, dst, target = (
            ((1, own), (cx + 1, own), (gx - 1, gy)),
            ((cx, own), (0, own), (gx + 1, gy)),
            ((rows, slice(lo, lo + 1)), (rows, slice(hi, hi + 1)), (gx, gy - 1)),
            ((rows, slice(hi - 1, hi)), (rows, slice(lo - 1, lo)), (gx, gy + 1)),
        )[way]
        return pltpu.make_async_remote_copy(
            src_ref=ref.at[lead + src],
            dst_ref=ref.at[lead + dst],
            send_sem=halo_send.at[step, way],
            recv_sem=halo_recv.at[step, way],
            device_id=target,
            device_id_type=MESH,
        )

    sends = (gx > 0, gx < ngx - 1, gy > 0, gy < ngy - 1)
    receives = (gx < ngx - 1, gx > 0, gy < ngy - 1, gy > 0)

    def send(step, ref, ways):
        for way in ways:

            @pl.when(sends[way])
            def _(way=way):
                halo_copy(step, ref, way).start()

    def receive(step, ref):
        for way in range(4):

            @pl.when(receives[way])
            def _(way=way):
                halo_copy(step, ref, way).wait_recv()

    def finish(step, ref):
        for way in range(4):

            @pl.when(sends[way])
            def _(way=way):
                halo_copy(step, ref, way).wait_send()

    lane = lax.broadcasted_iota(jnp.int32, (1, cz), 1)
    first_lane, last_lane = lane == 0, lane == cz - 1

    def along_depth(v):
        before = jnp.where(first_lane, 0.0, pltpu.roll(v, 1, axis=1))
        after = jnp.where(last_lane, 0.0, pltpu.roll(v, cz - 1, axis=1))
        return before, after

    def planes(first, last, together, work):
        def some(i, _):
            for k in range(together):
                work(first + i * together + k)
            return 0

        lax.fori_loop(0, (last - first) // together, some, 0)

    def start_plane(x):
        for c in range(2):
            part = 1.0 / (inv[c, x] + 6.0)
            inv[c, x] = part
            dir0[c, x + 1, lo:hi, :] = part * rhs[c, x] * (1.0 / THETA)

    for n, i in enumerate(chunk_order):
        for copy in load_chunk(i):
            copy.wait()
        planes(i * per, (i + 1) * per, 4, start_plane)
        if n == 4:
            pl.semaphore_wait(barrier, ndev - 1)
            send(0, dir0, (0, 1))
    send(0, dir0, (2, 3))
    load_cpl.wait()

    table, scales = recurrence()

    def sweep_rows(sweep, x, y, rows):
        now = (dir0, dir1, dir2)[sweep]
        of_now, of_before = table[sweep]
        at = pl.ds(lo + y, rows)
        mid = [now[c, x + 1, at, :] for c in range(2)]
        mix = cpl[x, pl.ds(y, rows), :]
        out = []
        for c in range(2):
            before, after = along_depth(mid[c])
            nbrs = now[c, x, at, :] + now[c, x + 2, at, :]
            nbrs = nbrs + now[c, x + 1, pl.ds(lo + y - 1, rows), :]
            nbrs = nbrs + now[c, x + 1, pl.ds(lo + y + 1, rows), :]
            nbrs = nbrs + (before + after)
            update = inv[c, x, pl.ds(y, rows), :] * (nbrs - mix * mid[1 - c])
            new = of_now * mid[c] + update
            if sweep > 0:
                new = new + of_before * (dir0, dir1)[sweep - 1][c, x + 1, at, :]
            out.append(new)
        if sweep < SWEEPS - 1:
            for c in range(2):
                (dir1, dir2)[sweep][c, x + 1, at, :] = out[c]
        else:
            for c in range(2):
                total = scales[0] * dir0[c, x + 1, at, :] + scales[1] * dir1[c, x + 1, at, :]
                total = total + (scales[2] * mid[c] + scales[3] * out[c])
                rhs[c, x, pl.ds(y, rows), :] = total
                if c == 0:
                    phase[x + 1, at, :] = pold[x, pl.ds(y, rows), :] + total

    for sweep in range(SWEEPS):
        now = (dir0, dir1, dir2)[sweep]
        new = (dir1, dir2, phase)[sweep]
        receive(sweep, now)
        if sweep == SWEEPS - 1:
            load_pold.wait()
        sweep_rows(sweep, 0, 0, cy)
        sweep_rows(sweep, cx - 1, 0, cy)
        send(sweep + 1, new, (0, 1))

        def edges(x, sweep=sweep):
            sweep_rows(sweep, x, 0, 8)
            sweep_rows(sweep, x, cy - 8, 8)

        sweep_rows(sweep, cx - 2, 0, cy)
        sweep_rows(sweep, cx - 3, 0, cy)
        planes(1, cx - 3, 12, edges)
        send(sweep + 1, new, (2, 3))
        planes(1, cx - 3, 6, lambda x, sweep=sweep: sweep_rows(sweep, x, 8, cy - 16))

    store_corr = pltpu.make_async_copy(rhs, corr_hbm, out_sem.at[0])
    store_corr.start()
    receive(SWEEPS, phase)

    wide = lax.broadcasted_iota(jnp.int32, (cy // 4, cz), 1)
    even = wide % 2 == 0
    half = cz // 2
    in_place = jnp.where(wide < half, 2 * wide, 2 * (wide - half) + 1)
    beside = jnp.where(wide < half, 2 * wide + 1, 2 * (wide - half))

    def pick(v, lanes):
        return jnp.take_along_axis(v, lanes, axis=1, mode="promise_in_bounds")

    def coarse_plane(i):
        sums = [None] * 4
        for x in (2 * i, 2 * i + 1):
            at = pl.ds(lo, cy)
            mid = phase[x + 1, at, :]
            weight = 0.0625 * rhs[1, x]
            before, after = along_depth(mid)
            fields = (
                mid,
                weight * (phase[x + 2, at, :] - phase[x, at, :]),
                weight * (phase[x + 1, pl.ds(lo + 1, cy), :] - phase[x + 1, pl.ds(lo - 1, cy), :]),
                weight * (after - before),
            )
            sums = [f if s is None else s + f for s, f in zip(sums, fields)]
        sums[0] = 0.125 * sums[0]
        quarter = cy // 4
        for f in range(4):
            slab[lax.rem(i, 4), f] = sums[f]
        for f in range(4):
            part = [slab[lax.rem(i, 4), f, pl.ds(k, quarter, stride=4), :] for k in range(4)]
            left, right = part[0] + part[1], part[2] + part[3]
            mean = pick(jnp.where(even, left, right), in_place)
            mean = mean + pick(jnp.where(even, right, left), beside)
            for q in range(4):
                packed[i * 4 + q, f * 4 : f * 4 + 4, :] = mean[q * 4 : q * 4 + 4, :]

    planes(0, cx // 2, 4, coarse_plane)

    def unit_copy(peer):
        return pltpu.make_async_remote_copy(
            src_ref=stage.at[peer],
            dst_ref=recv.at[pl.ds(me * unit_rows, unit_rows)],
            send_sem=unit_send,
            recv_sem=unit_recv,
            device_id=(peer // ngy, lax.rem(peer, ngy)),
            device_id_type=MESH,
        )

    def ship(k, _):
        peer = lax.rem(me + k, ndev)
        stage[peer] = packed[order[peer]]
        unit_copy(peer).start()
        return 0

    lax.fori_loop(1, ndev, ship, 0)
    recv[pl.ds(me * unit_rows, unit_rows), :] = packed[order[me]]

    for step, ref in enumerate((dir0, dir1, dir2, phase)):
        finish(step, ref)
    load_vel.wait()
    others = pl.ds(0, (ndev - 1) * unit_rows)
    pltpu.make_async_copy(recv.at[others], recv.at[others], unit_recv).wait()

    place = lax.rem(lane, cz // 2)
    bottom, top = place == 0, place == cz // 2 - 1

    def product(v, density, visc, weight):
        below = jnp.where(bottom, 0.0, pltpu.roll(v, 1, axis=1))
        flux = weight * (v - below)
        above = jnp.where(top, -visc * v, pltpu.roll(flux, cz - 1, axis=1))
        return density * v - (above - flux)

    for r in range(4):
        get = lambda f: recv[pl.ds(f * 4 + r, ndev, stride=unit_rows), :]
        mean = get(0)
        density = 0.1 + 0.45 * (1.0 + mean)
        visc = 0.2 + 0.4 * (1.0 + mean)
        weight = 0.5 * (visc + jnp.where(bottom, visc, pltpu.roll(visc, 1, axis=1)))
        for c in range(3):
            at = pl.ds(r * cz, cz)
            stress = product(vel[c, :, at], density, visc, weight) - get(c + 1)
            mom[c, :, at] = product(stress, density, visc, weight)

    store_mom = pltpu.make_async_copy(mom, mom_hbm, out_sem.at[1])
    store_mom.start()
    sent = pl.ds(0, ndev - 1)
    pltpu.make_async_copy(stage.at[sent], stage.at[sent], unit_send).wait()
    store_corr.wait()
    store_mom.wait()


def body(ngx, ngy, right_side, well_coef, mobility_coef, coupling, phase_old, unit_owner, velocity):
    _, cx, cy, cz = right_side.shape
    ndev = ngx * ngy
    chunks = 8
    unit_rows = 4 * (velocity.shape[2] // cz)
    ids = jnp.arange(ndev, dtype=jnp.int32)
    order = jnp.sum(jnp.where(unit_owner[None, :] == ids[:, None], ids[None, :], 0), axis=1)
    any_spec = pl.BlockSpec(memory_space=pl.ANY)
    padded = (cx + 2, cy + 2 * PAD, cz)
    f32 = jnp.float32
    return pl.pallas_call(
        functools.partial(kernel_body, (ngx, ngy, cx, cy, cz, chunks)),
        out_shape=(
            jax.ShapeDtypeStruct(right_side.shape, f32),
            jax.ShapeDtypeStruct(velocity.shape, f32),
        ),
        in_specs=[pl.BlockSpec(memory_space=pltpu.SMEM)] + [any_spec] * 6,
        out_specs=(any_spec, any_spec),
        scratch_shapes=[
            pltpu.VMEM((2, cx, cy, cz), f32),
            pltpu.VMEM((2, cx, cy, cz), f32),
            pltpu.VMEM((cx, cy, cz), f32),
            pltpu.VMEM((cx, cy, cz), f32),
            pltpu.VMEM((2,) + padded, f32),
            pltpu.VMEM((2,) + padded, f32),
            pltpu.VMEM((2,) + padded, f32),
            pltpu.VMEM(padded, f32),
            pltpu.VMEM((4, 4, cy, cz), f32),
            pltpu.VMEM((ndev, unit_rows, cz), f32),
            pltpu.VMEM((ndev, unit_rows, cz), f32),
            pltpu.VMEM((ndev * unit_rows, cz), f32),
            pltpu.VMEM(velocity.shape, f32),
            pltpu.VMEM(velocity.shape, f32),
            pltpu.SemaphoreType.DMA((chunks, 3)),
            pltpu.SemaphoreType.DMA((3,)),
            pltpu.SemaphoreType.DMA((2,)),
            pltpu.SemaphoreType.DMA((SWEEPS + 1, 4)),
            pltpu.SemaphoreType.DMA((SWEEPS + 1, 4)),
            pltpu.SemaphoreType.DMA,
            pltpu.SemaphoreType.DMA,
        ],
        compiler_params=pltpu.CompilerParams(
            collective_id=0, has_side_effects=True, vmem_limit_bytes=56 * 1024 * 1024
        ),
    )(order, right_side, well_coef, mobility_coef, coupling, phase_old, velocity)


def solution(mesh):
    return jax.shard_map(
        functools.partial(body, mesh.shape["gx"], mesh.shape["gy"]),
        mesh=mesh,
        in_specs=(
            P(None, "gx", "gy", None),
            P("gx", "gy", None),
            P("gx", "gy", None),
            P("gx", "gy", None),
            P("gx", "gy", None),
            P(("gx", "gy")),
            P(None, ("gx", "gy"), None),
        ),
        out_specs=(P(None, "gx", "gy", None), P(None, ("gx", "gy"), None)),
        check_vma=False,
    )
```

```python
import functools

import jax
import jax.numpy as jnp
from jax import lax
from jax.experimental import pallas as pl
from jax.experimental.pallas import tpu as pltpu
from jax.sharding import PartitionSpec as P

SWEEPS = 3
LOW_BOUND = 0.15
HIGH_BOUND = 1.85
THETA = (HIGH_BOUND + LOW_BOUND) / 2.0
DELTA = (HIGH_BOUND - LOW_BOUND) / 2.0
SIGMA = THETA / DELTA

PAD = 8
MESH = pl.DeviceIdType.MESH


def recurrence():
    table, scales = [], [1.0]
    rho = 1.0 / SIGMA
    decay_before, gain_before = 0.0, 0.0
    for sweep in range(SWEEPS):
        rho_new = 1.0 / (2.0 * SIGMA - rho)
        decay, gain = rho_new * rho, 2.0 * rho_new / DELTA
        if sweep == 0:
            table.append(((decay + gain * (THETA - 1.0)) / gain, 0.0))
        else:
            ratio = gain / gain_before
            before = -ratio * decay_before * scales[-2] / (gain * scales[-1])
            table.append(((decay + ratio - gain) / gain, before))
        scales.append(scales[-1] * gain)
        decay_before, gain_before, rho = decay, gain, rho_new
    return table, scales


def kernel_body(
    sizes,
    owner,
    rhs_hbm,
    well_hbm,
    mob_hbm,
    cpl_hbm,
    pold_hbm,
    vel_hbm,
    corr,
    mom,
    owner_row,
    order_row,
    order,
    inv,
    inv_edge,
    cpl,
    pold,
    dir0,
    dir1,
    dir2,
    phase,
    x_recv,
    y_send,
    y_recv,
    slab,
    packed,
    stage,
    recv,
    vel,
    load_sem,
    rest_sem,
    halo_send,
    halo_recv,
    unit_send,
    unit_recv,
):
    ngx, ngy, cx, cy, cz, chunks = sizes
    ndev = ngx * ngy
    gx, gy = lax.axis_index("gx"), lax.axis_index("gy")
    me = gx * ngy + gy
    per = cx // chunks
    pitch = cy + 2 * PAD
    f32 = jnp.float32

    def padded(x, rows=cy):
        return pl.ds(pl.multiple_of((x + 1) * pitch + PAD, 8), rows)

    def shifted(x, by):
        return pl.ds((x + 1) * pitch + PAD + by, cy)

    def plain(x):
        return pl.ds(pl.multiple_of(x * cy, 8), cy)

    def padded_column(y):
        return pl.ds(pitch + PAD + y, cx, stride=pitch)

    def plain_column(y):
        return pl.ds(y, cx, stride=cy)

    ends_x, ends_y = (0, cx - 1), (0, cy - 1)

    def load_chunk(i):
        at = pl.ds(i * per * cy, per * cy)
        return (
            pltpu.make_async_copy(rhs_hbm.at[:, at], corr.at[:, at], load_sem.at[i, 0]),
            pltpu.make_async_copy(well_hbm.at[at], inv.at[0, at], load_sem.at[i, 1]),
            pltpu.make_async_copy(mob_hbm.at[at], inv.at[1, at], load_sem.at[i, 2]),
        )

    load_cpl = pltpu.make_async_copy(cpl_hbm, cpl, rest_sem.at[0])
    load_pold = pltpu.make_async_copy(pold_hbm, pold, rest_sem.at[1])
    load_vel = pltpu.make_async_copy(vel_hbm, vel, rest_sem.at[2])
    load_owner = pltpu.make_async_copy(owner, owner_row, rest_sem.at[4])
    load_owner.start()
    chunk_order = [0, chunks - 1] + list(range(1, chunks - 1))
    for i in chunk_order:
        for copy in load_chunk(i):
            copy.start()
    load_cpl.start()
    load_pold.start()
    load_vel.start()

    barrier = pltpu.get_barrier_semaphore()

    def greet(k, _):
        peer = lax.rem(me + k, ndev)
        pl.semaphore_signal(
            barrier, inc=1, device_id=(peer // ngy, lax.rem(peer, ngy)), device_id_type=MESH
        )
        return 0

    lax.fori_loop(1, ndev, greet, 0)

    down = lax.broadcasted_iota(jnp.int32, (ndev, ndev), 0)
    across = lax.broadcasted_iota(jnp.int32, (ndev, ndev), 1)
    load_owner.wait()
    unit_of = jnp.max(jnp.where(owner_row[...] == down, across, 0), axis=1, keepdims=True)
    order_row[...] = jnp.max(jnp.where(down == across, unit_of, 0), axis=0, keepdims=True)
    save_order = pltpu.make_async_copy(order_row, order, rest_sem.at[3])
    save_order.start()

    for buf in (dir0, dir1, dir2):
        for c in range(2):
            for x in (-1, cx):
                buf[c, padded(x), :] = jnp.zeros((cy, cz), f32)
            for y in (-1, cy):
                buf[c, padded_column(y), :] = jnp.zeros((cx, cz), f32)
    for y in (-1, cy):
        phase[padded_column(y), :] = jnp.zeros((cx, cz), f32)

    @pl.when(gx == 0)
    def _():
        phase[padded(-1), :] = jnp.zeros((cy, cz), f32)

    @pl.when(gx == ngx - 1)
    def _():
        phase[padded(cx), :] = jnp.zeros((cy, cz), f32)

    targets = ((gx - 1, gy), (gx + 1, gy), (gx, gy - 1), (gx, gy + 1))
    sends = (gx > 0, gx < ngx - 1, gy > 0, gy < ngy - 1)

    def halo_copy(step, way):
        side, other = way % 2, 1 - way % 2
        if way >= 2:
            src, dst = y_send.at[step, side], y_recv.at[step, other]
            if step == SWEEPS:
                src, dst = src.at[0], dst.at[0]
        elif step == SWEEPS:
            src, dst = phase.at[padded(ends_x[side])], phase.at[padded((-1, cx)[other])]
        else:
            src = (dir0, dir1, dir2)[step].at[:, padded(ends_x[side])]
            dst = x_recv.at[step, other]
        return pltpu.make_async_remote_copy(
            src_ref=src,
            dst_ref=dst,
            send_sem=halo_send.at[step, way],
            recv_sem=halo_recv.at[step, way],
            device_id=targets[way],
            device_id_type=MESH,
        )

    def send(step, ways):
        for way in ways:

            @pl.when(sends[way])
            def _(way=way):
                halo_copy(step, way).start()

    def receive(step, way, work):
        @pl.when(sends[way ^ 1])
        def _():
            halo_copy(step, way).wait_recv()
            work()

    def finish(step):
        for way in range(4):

            @pl.when(sends[way])
            def _(way=way):
                halo_copy(step, way).wait_send()

    lane = lax.broadcasted_iota(jnp.int32, (1, cz), 1)
    first_lane, last_lane = lane == 0, lane == cz - 1

    def along_depth(v):
        before = jnp.where(first_lane, 0.0, pltpu.roll(v, 1, axis=1))
        after = jnp.where(last_lane, 0.0, pltpu.roll(v, cz - 1, axis=1))
        return before, after

    def planes(first, last, together, work):
        def some(i, _):
            for k in range(together):
                work(first + i * together + k)
            return 0

        lax.fori_loop(0, (last - first) // together, some, 0)

    def start_plane(x):
        for c in range(2):
            part = 1.0 / (inv[c, plain(x), :] + 6.0)
            inv[c, plain(x), :] = part
            dir0[c, padded(x), :] = part * corr[c, plain(x), :] * (1.0 / THETA)

    for n, i in enumerate(chunk_order):
        for copy in load_chunk(i):
            copy.wait()
        planes(i * per, (i + 1) * per, 4, start_plane)
        if n == 4:
            pl.semaphore_wait(barrier, ndev - 1)
            send(0, (0, 1))
    for side in range(2):
        for c in range(2):
            y_send[0, side, c] = dir0[c, padded_column(ends_y[side]), :]
    send(0, (2, 3))
    for side in range(2):
        for c in range(2):
            inv_edge[side, c] = inv[c, plain_column(ends_y[side]), :]
    load_cpl.wait()

    table, scales = recurrence()

    def own(x, y, rows):
        return pl.ds(pl.multiple_of((x + 1) * pitch + PAD + y, 8), rows)

    def sweep_plane(sweep, x, y, rows):
        now = (dir0, dir1, dir2)[sweep]
        of_now, of_before = table[sweep]
        mid = [now[c, own(x, y, rows), :] for c in range(2)]
        mix = cpl[pl.ds(pl.multiple_of(x * cy + y, 8), rows), :]
        for c in range(2):
            before, after = along_depth(mid[c])
            nbrs = now[c, own(x - 1, y, rows), :] + now[c, own(x + 1, y, rows), :]
            nbrs = nbrs + (now[c, pl.ds((x + 1) * pitch + PAD + y - 1, rows), :] + now[c, pl.ds((x + 1) * pitch + PAD + y + 1, rows), :])
            nbrs = nbrs + (before + after)
            new = of_now * mid[c] + inv[c, pl.ds(pl.multiple_of(x * cy + y, 8), rows), :] * (nbrs - mix * mid[1 - c])
            if sweep > 0:
                new = new + of_before * (dir0, dir1)[sweep - 1][c, own(x, y, rows), :]
            if sweep < SWEEPS - 1:
                (dir1, dir2)[sweep][c, own(x, y, rows), :] = new
            else:
                total = scales[0] * dir0[c, own(x, y, rows), :] + scales[1] * dir1[c, own(x, y, rows), :]
                total = total + (scales[2] * mid[c] + scales[3] * new)
                corr[c, pl.ds(pl.multiple_of(x * cy + y, 8), rows), :] = total
                if c == 0:
                    phase[own(x, y, rows), :] = pold[pl.ds(pl.multiple_of(x * cy + y, 8), rows), :] + total

    def add_halos(sweep):
        last = sweep == SWEEPS - 1
        into = None if last else (dir1, dir2)[sweep]
        for side in range(2):

            def along_x(side=side):
                x = ends_x[side]
                for c in range(2):
                    more = inv[c, plain(x), :] * x_recv[sweep, side, c]
                    if last:
                        corr[c, plain(x), :] += scales[3] * more
                        if c == 0:
                            phase[padded(x), :] += scales[3] * more
                    else:
                        into[c, padded(x), :] += more

            receive(sweep, 1 - side, along_x)
        for side in range(2):

            def along_y(side=side):
                y = ends_y[side]
                for c in range(2):
                    more = inv_edge[side, c] * y_recv[sweep, side, c]
                    if last:
                        corr[c, plain_column(y), :] += scales[3] * more
                        if c == 0:
                            phase[padded_column(y), :] += scales[3] * more
                    else:
                        into[c, padded_column(y), :] += more

            receive(sweep, 3 - side, along_y)
        send(sweep + 1, (0, 1))
        for side in range(2):
            if last:
                y_send[sweep + 1, side, 0] = phase[padded_column(ends_y[side]), :]
            else:
                for c in range(2):
                    y_send[sweep + 1, side, c] = into[c, padded_column(ends_y[side]), :]
        send(sweep + 1, (2, 3))

    for sweep in range(SWEEPS):
        if sweep == SWEEPS - 1:
            load_pold.wait()
        def plane(x, sweep=sweep):
            for y in range(0, cy, 32):
                sweep_plane(sweep, x, y, 32)

        planes(0, cx, 4, plane)
        add_halos(sweep)

    wide = lax.broadcasted_iota(jnp.int32, (cy // 4, cz), 1)
    even = wide % 2 == 0
    half = cz // 2
    in_place = jnp.where(wide < half, 2 * wide, 2 * (wide - half) + 1)
    beside = jnp.where(wide < half, 2 * wide + 1, 2 * (wide - half))

    def pick(v, lanes):
        return jnp.take_along_axis(v, lanes, axis=1, mode="promise_in_bounds")

    def coarse_plane(part, i):
        sums = [None] * 2
        for x in (2 * i, 2 * i + 1):
            weight = 0.0625 * corr[1, plain(x), :]
            if part == 0:
                mid = phase[padded(x), :]
                before, after = along_depth(mid)
                fields = (0.125 * mid, weight * (after - before))
            else:
                fields = (
                    weight * (phase[padded(x + 1), :] - phase[padded(x - 1), :]),
                    weight * (phase[shifted(x, 1), :] - phase[shifted(x, -1), :]),
                )
            sums = [f if s is None else s + f for s, f in zip(sums, fields)]
        quarter = cy // 4
        slot = lax.rem(i, 4)
        for f in range(2):
            slab[slot, f] = sums[f]
        for f in range(2):
            rows = [slab[slot, f, pl.ds(k, quarter, stride=4), :] for k in range(4)]
            left, right = rows[0] + rows[1], rows[2] + rows[3]
            mean = pick(jnp.where(even, left, right), in_place)
            mean = mean + pick(jnp.where(even, right, left), beside)
            for q in range(4):
                packed[part, i * 4 + q, f * 4 : f * 4 + 4, :] = mean[q * 4 : q * 4 + 4, :]

    unit_rows = packed.shape[2]

    def unit_copy(part, peer):
        return pltpu.make_async_remote_copy(
            src_ref=stage.at[part, peer],
            dst_ref=recv.at[part, pl.ds(me * unit_rows, unit_rows)],
            send_sem=unit_send.at[part],
            recv_sem=unit_recv.at[part],
            device_id=(peer // ngy, lax.rem(peer, ngy)),
            device_id_type=MESH,
        )

    def ship(part):
        def one(k):
            peer = lax.rem(me + k, ndev)
            stage[part, peer] = packed[part, order[0, peer]]
            unit_copy(part, peer).start()

        planes(1, ndev - 1, 6, one)
        one(ndev - 1)
        recv[part, pl.ds(me * unit_rows, unit_rows), :] = packed[part, order[0, me]]

    def arrive(part):
        others = recv.at[part, pl.ds(0, (ndev - 1) * unit_rows)]
        pltpu.make_async_copy(others, others, unit_recv.at[part]).wait()

    save_order.wait()
    planes(0, cx // 2, 4, functools.partial(coarse_plane, 0))
    ship(0)
    for way in range(2):
        receive(SWEEPS, way, lambda: None)
    for side in range(2):

        def beyond(side=side):
            phase[padded_column((-1, cy)[side]), :] = y_recv[SWEEPS, side, 0]

        receive(SWEEPS, 3 - side, beyond)
    planes(0, cx // 2, 4, functools.partial(coarse_plane, 1))
    ship(1)

    for step in range(SWEEPS + 1):
        finish(step)
    load_vel.wait()

    place = lax.rem(lane, cz // 2)
    bottom, top = place == 0, place == cz // 2 - 1

    def product(v, density, visc, weight):
        below = jnp.where(bottom, 0.0, pltpu.roll(v, 1, axis=1))
        flux = weight * (v - below)
        above = jnp.where(top, -visc * v, pltpu.roll(flux, cz - 1, axis=1))
        return density * v - (above - flux)

    def get(part, f, r):
        return recv[part, pl.ds(f * 4 + r, ndev, stride=unit_rows), :]

    def factors(r):
        mean = get(0, 0, r)
        density = 0.1 + 0.45 * (1.0 + mean)
        visc = 0.2 + 0.4 * (1.0 + mean)
        weight = 0.5 * (visc + jnp.where(bottom, visc, pltpu.roll(visc, 1, axis=1)))
        return density, visc, weight

    arrive(0)
    for r in range(4):
        at = pl.ds(r * cz, cz)
        parts = factors(r)
        for c in range(3):
            stress = product(vel[c, :, at], *parts)
            mom[c, :, at] = product(stress - get(0, 1, r), *parts) if c == 2 else stress
    arrive(1)
    for r in range(4):
        at = pl.ds(r * cz, cz)
        parts = factors(r)
        for c in range(2):
            mom[c, :, at] = product(mom[c, :, at] - get(1, c, r), *parts)

    for part in range(2):
        sent = stage.at[part, pl.ds(0, ndev - 1)]
        pltpu.make_async_copy(sent, sent, unit_send.at[part]).wait()


def body(ngx, ngy, right_side, well_coef, mobility_coef, coupling, phase_old, unit_owner, velocity):
    _, cx, cy, cz = right_side.shape
    ndev = ngx * ngy
    chunks = 8
    unit_rows = 2 * (velocity.shape[2] // cz)
    flat = cx * cy
    padded = (cx + 2) * (cy + 2 * PAD)
    hbm_spec = pl.BlockSpec(memory_space=pltpu.HBM)
    vmem_spec = pl.BlockSpec(memory_space=pltpu.VMEM)
    f32 = jnp.float32
    steps = SWEEPS + 1
    hbm = lambda x: pltpu.with_memory_space_constraint(x, pltpu.HBM)
    correction, momentum = pl.pallas_call(
        functools.partial(kernel_body, (ngx, ngy, cx, cy, cz, chunks)),
        out_shape=(
            pltpu.VMEM((2, flat, cz), f32),
            pltpu.VMEM(velocity.shape, f32),
        ),
        in_specs=[hbm_spec] * 7,
        out_specs=(vmem_spec, vmem_spec),
        scratch_shapes=[
            pltpu.VMEM((1, ndev), jnp.int32),
            pltpu.VMEM((1, ndev), jnp.int32),
            pltpu.SMEM((1, ndev), jnp.int32),
            pltpu.VMEM((2, flat, cz), f32),
            pltpu.VMEM((2, 2, cx, cz), f32),
            pltpu.VMEM((flat, cz), f32),
            pltpu.VMEM((flat, cz), f32),
            pltpu.VMEM((2, padded, cz), f32),
            pltpu.VMEM((2, padded, cz), f32),
            pltpu.VMEM((2, padded, cz), f32),
            pltpu.VMEM((padded, cz), f32),
            pltpu.VMEM((SWEEPS, 2, 2, cy, cz), f32),
            pltpu.VMEM((steps, 2, 2, cx, cz), f32),
            pltpu.VMEM((steps, 2, 2, cx, cz), f32),
            pltpu.VMEM((4, 2, cy, cz), f32),
            pltpu.VMEM((2, ndev, unit_rows, cz), f32),
            pltpu.VMEM((2, ndev, unit_rows, cz), f32),
            pltpu.VMEM((2, ndev * unit_rows, cz), f32),
            pltpu.VMEM(velocity.shape, f32),
            pltpu.SemaphoreType.DMA((chunks, 3)),
            pltpu.SemaphoreType.DMA((5,)),
            pltpu.SemaphoreType.DMA((steps, 4)),
            pltpu.SemaphoreType.DMA((steps, 4)),
            pltpu.SemaphoreType.DMA((2,)),
            pltpu.SemaphoreType.DMA((2,)),
        ],
        compiler_params=pltpu.CompilerParams(
            collective_id=0, has_side_effects=True, vmem_limit_bytes=48 * 1024 * 1024
        ),
    )(
        hbm(unit_owner.reshape(1, ndev)),
        hbm(right_side.reshape(2, flat, cz)),
        hbm(well_coef.reshape(flat, cz)),
        hbm(mobility_coef.reshape(flat, cz)),
        hbm(coupling.reshape(flat, cz)),
        hbm(phase_old.reshape(flat, cz)),
        hbm(velocity),
    )
    return correction.reshape(right_side.shape), momentum


def solution(mesh):
    return jax.shard_map(
        functools.partial(body, mesh.shape["gx"], mesh.shape["gy"]),
        mesh=mesh,
        in_specs=(
            P(None, "gx", "gy", None),
            P("gx", "gy", None),
            P("gx", "gy", None),
            P("gx", "gy", None),
            P("gx", "gy", None),
            P(("gx", "gy")),
            P(None, ("gx", "gy"), None),
        ),
        out_specs=(P(None, "gx", "gy", None), P(None, ("gx", "gy"), None)),
        check_vma=False,
    )
```

```python
import functools

import jax
import jax.numpy as jnp
from jax import lax
from jax.experimental import pallas as pl
from jax.experimental.pallas import tpu as pltpu
from jax.sharding import PartitionSpec as P

SWEEPS = 3
LOW_BOUND = 0.15
HIGH_BOUND = 1.85
THETA = (HIGH_BOUND + LOW_BOUND) / 2.0
DELTA = (HIGH_BOUND - LOW_BOUND) / 2.0
SIGMA = THETA / DELTA

PAD = 8
OUT_PIECES = 4
MESH = pl.DeviceIdType.MESH
FLAT = pl.DeviceIdType.LOGICAL


def recurrence():
    table, scales = [], [1.0]
    rho = 1.0 / SIGMA
    decay_before, gain_before = 0.0, 0.0
    for sweep in range(SWEEPS):
        rho_new = 1.0 / (2.0 * SIGMA - rho)
        decay, gain = rho_new * rho, 2.0 * rho_new / DELTA
        if sweep == 0:
            table.append(((decay + gain * (THETA - 1.0)) / gain, 0.0))
        else:
            ratio = gain / gain_before
            before = -ratio * decay_before * scales[-2] / (gain * scales[-1])
            table.append(((decay + ratio - gain) / gain, before))
        scales.append(scales[-1] * gain)
        decay_before, gain_before, rho = decay, gain, rho_new
    return table, scales


def column_products(cz, recv):
    unit_rows = 8
    units = recv.shape[1] // unit_rows
    lane = lax.broadcasted_iota(jnp.int32, (1, cz), 1)
    place = lax.rem(lane, cz // 2)
    bottom, top = place == 0, place == cz // 2 - 1

    def product(v, density, visc, weight):
        below = jnp.where(bottom, 0.0, pltpu.roll(v, 1, axis=1))
        flux = weight * (v - below)
        above = jnp.where(top, -visc * v, pltpu.roll(flux, cz - 1, axis=1))
        return density * v - (above - flux)

    def get(part, f, r):
        return recv[part, pl.ds(f * 4 + r, units, stride=unit_rows), :]

    def factors(r):
        mean = get(0, 0, r)
        density = 0.1 + 0.45 * (1.0 + mean)
        visc = 0.2 + 0.4 * (1.0 + mean)
        weight = 0.5 * (visc + jnp.where(bottom, visc, pltpu.roll(visc, 1, axis=1)))
        return density, visc, weight

    return product, get, factors


def kernel_body(
    sizes,
    owner,
    rhs_hbm,
    well_hbm,
    mob_hbm,
    cpl_hbm,
    pold_hbm,
    vel_hbm,
    rhs_rows,
    well_rows,
    mob_rows,
    corr,
    mom,
    recv,
    owner_row,
    order_row,
    order,
    inv,
    rhs_edge,
    inv_edge,
    cpl,
    pold,
    dir0,
    dir1,
    dir2,
    phase,
    x_recv,
    y_send,
    y_recv,
    slab,
    packed,
    stage,
    vel,
    load_sem,
    edge_sem,
    rest_sem,
    halo_send,
    halo_recv,
    unit_send,
    unit_recv,
):
    ngx, ngy, cx, cy, cz, chunks = sizes
    ndev = ngx * ngy
    gx, gy = lax.axis_index("gx"), lax.axis_index("gy")
    me = gx * ngy + gy
    per = cx // chunks
    pitch = cy + 2 * PAD
    f32 = jnp.float32

    def planes(first, last, together, work):
        def some(i, _):
            for k in range(together):
                work(first + i * together + k)
            return 0

        lax.fori_loop(0, (last - first) // together, some, 0)

    def padded(x, rows=cy):
        return pl.ds(pl.multiple_of((x + 1) * pitch + PAD, 8), rows)

    def shifted(x, by):
        return pl.ds((x + 1) * pitch + PAD + by, cy)

    def plain(x):
        return pl.ds(pl.multiple_of(x * cy, 8), cy)

    def padded_column(y):
        return pl.ds(pitch + PAD + y, cx, stride=pitch)

    def plain_column(y):
        return pl.ds(y, cx, stride=cy)

    ends_x, ends_y = (0, cx - 1), (0, cy - 1)

    barrier = pltpu.get_barrier_semaphore()

    def greet(k):
        pl.semaphore_signal(
            barrier, inc=1, device_id=lax.rem(me + k, ndev), device_id_type=FLAT
        )

    planes(1, ndev - 1, 9, greet)
    greet(ndev - 1)

    def load_chunk(i):
        at = pl.ds(i * per * cy, per * cy)
        return (
            pltpu.make_async_copy(rhs_hbm.at[:, at], corr.at[:, at], load_sem.at[i, 0]),
            pltpu.make_async_copy(well_hbm.at[at], inv.at[0, at], load_sem.at[i, 1]),
            pltpu.make_async_copy(mob_hbm.at[at], inv.at[1, at], load_sem.at[i, 2]),
        )

    def load_edge(side):
        y = ends_y[side]
        return (
            pltpu.make_async_copy(rhs_rows.at[:, :, y], rhs_edge.at[side], edge_sem.at[side, 0]),
            pltpu.make_async_copy(well_rows.at[:, y], inv_edge.at[side, 0], edge_sem.at[side, 1]),
            pltpu.make_async_copy(mob_rows.at[:, y], inv_edge.at[side, 1], edge_sem.at[side, 2]),
        )

    load_cpl = pltpu.make_async_copy(cpl_hbm, cpl, rest_sem.at[0])
    load_pold = pltpu.make_async_copy(pold_hbm, pold, rest_sem.at[1])
    load_vel = pltpu.make_async_copy(vel_hbm, vel, rest_sem.at[2])
    load_owner = pltpu.make_async_copy(owner, owner_row, rest_sem.at[4])
    load_owner.start()
    chunk_order = [0, chunks - 1] + list(range(1, chunks - 1))
    for side in range(2):
        for copy in load_edge(side):
            copy.start()
    for i in chunk_order:
        for copy in load_chunk(i):
            copy.start()
    load_cpl.start()
    load_pold.start()
    load_vel.start()

    down = lax.broadcasted_iota(jnp.int32, (ndev, ndev), 0)
    across = lax.broadcasted_iota(jnp.int32, (ndev, ndev), 1)
    load_owner.wait()
    unit_of = jnp.max(jnp.where(owner_row[...] == down, across, 0), axis=1, keepdims=True)
    order_row[...] = jnp.max(jnp.where(down == across, unit_of, 0), axis=0, keepdims=True)
    save_order = pltpu.make_async_copy(order_row, order, rest_sem.at[3])
    save_order.start()

    for buf in (dir0, dir1, dir2):
        for c in range(2):
            for x in (-1, cx):
                buf[c, padded(x), :] = jnp.zeros((cy, cz), f32)
            for y in (-1, cy):
                buf[c, padded_column(y), :] = jnp.zeros((cx, cz), f32)
    for y in (-1, cy):
        phase[padded_column(y), :] = jnp.zeros((cx, cz), f32)

    @pl.when(gx == 0)
    def _():
        phase[padded(-1), :] = jnp.zeros((cy, cz), f32)

    @pl.when(gx == ngx - 1)
    def _():
        phase[padded(cx), :] = jnp.zeros((cy, cz), f32)

    targets = ((gx - 1, gy), (gx + 1, gy), (gx, gy - 1), (gx, gy + 1))
    sends = (gx > 0, gx < ngx - 1, gy > 0, gy < ngy - 1)

    def halo_copy(step, way):
        side, other = way % 2, 1 - way % 2
        if way >= 2:
            src, dst = y_send.at[step, side], y_recv.at[step, other]
            if step == SWEEPS:
                src, dst = src.at[0], dst.at[0]
        elif step == SWEEPS:
            src, dst = phase.at[padded(ends_x[side])], phase.at[padded((-1, cx)[other])]
        else:
            src = (dir0, dir1, dir2)[step].at[:, padded(ends_x[side])]
            dst = x_recv.at[step, other]
        return pltpu.make_async_remote_copy(
            src_ref=src,
            dst_ref=dst,
            send_sem=halo_send.at[step, way],
            recv_sem=halo_recv.at[step, way],
            device_id=targets[way],
            device_id_type=MESH,
        )

    def send(step, ways):
        for way in ways:

            @pl.when(sends[way])
            def _(way=way):
                halo_copy(step, way).start()

    def receive(step, way, work):
        @pl.when(sends[way ^ 1])
        def _():
            halo_copy(step, way).wait_recv()
            work()

    def finish(step):
        for way in range(4):

            @pl.when(sends[way])
            def _(way=way):
                halo_copy(step, way).wait_send()

    lane = lax.broadcasted_iota(jnp.int32, (1, cz), 1)
    first_lane, last_lane = lane == 0, lane == cz - 1

    def along_depth(v):
        before = jnp.where(first_lane, 0.0, pltpu.roll(v, 1, axis=1))
        after = jnp.where(last_lane, 0.0, pltpu.roll(v, cz - 1, axis=1))
        return before, after

    def start_plane(x):
        for c in range(2):
            part = 1.0 / (inv[c, plain(x), :] + 6.0)
            inv[c, plain(x), :] = part
            dir0[c, padded(x), :] = part * corr[c, plain(x), :] * (1.0 / THETA)

    for side in range(2):
        for copy in load_edge(side):
            copy.wait()
        for c in range(2):
            part = 1.0 / (inv_edge[side, c] + 6.0)
            inv_edge[side, c] = part
            y_send[0, side, c] = part * rhs_edge[side, c] * (1.0 / THETA)
    for n, i in enumerate(chunk_order):
        for copy in load_chunk(i):
            copy.wait()
        planes(i * per, (i + 1) * per, 4, start_plane)
        if n == 1:
            pl.semaphore_wait(barrier, ndev - 1)
            send(0, (0, 1, 2, 3))
    load_cpl.wait()

    table, scales = recurrence()

    def own(x, y, rows):
        return pl.ds(pl.multiple_of((x + 1) * pitch + PAD + y, 8), rows)

    def sweep_plane(sweep, x, y, rows):
        now = (dir0, dir1, dir2)[sweep]
        of_now, of_before = table[sweep]
        mid = [now[c, own(x, y, rows), :] for c in range(2)]
        mix = cpl[pl.ds(pl.multiple_of(x * cy + y, 8), rows), :]
        for c in range(2):
            before, after = along_depth(mid[c])
            nbrs = now[c, own(x - 1, y, rows), :] + now[c, own(x + 1, y, rows), :]
            nbrs = nbrs + (now[c, pl.ds((x + 1) * pitch + PAD + y - 1, rows), :] + now[c, pl.ds((x + 1) * pitch + PAD + y + 1, rows), :])
            nbrs = nbrs + (before + after)
            new = of_now * mid[c] + inv[c, pl.ds(pl.multiple_of(x * cy + y, 8), rows), :] * (nbrs - mix * mid[1 - c])
            if sweep > 0:
                new = new + of_before * (dir0, dir1)[sweep - 1][c, own(x, y, rows), :]
            if sweep < SWEEPS - 1:
                (dir1, dir2)[sweep][c, own(x, y, rows), :] = new
            else:
                total = scales[0] * dir0[c, own(x, y, rows), :] + scales[1] * dir1[c, own(x, y, rows), :]
                total = total + (scales[2] * mid[c] + scales[3] * new)
                corr[c, pl.ds(pl.multiple_of(x * cy + y, 8), rows), :] = total
                if c == 0:
                    phase[own(x, y, rows), :] = pold[pl.ds(pl.multiple_of(x * cy + y, 8), rows), :] + total

    def add_halos(sweep):
        last = sweep == SWEEPS - 1
        into = None if last else (dir1, dir2)[sweep]
        for side in range(2):

            def along_x(side=side):
                x = ends_x[side]
                for c in range(2):
                    more = inv[c, plain(x), :] * x_recv[sweep, side, c]
                    if last:
                        corr[c, plain(x), :] += scales[3] * more
                        if c == 0:
                            phase[padded(x), :] += scales[3] * more
                    else:
                        into[c, padded(x), :] += more

            receive(sweep, 1 - side, along_x)
        for side in range(2):

            def along_y(side=side):
                y = ends_y[side]
                for c in range(2):
                    more = inv_edge[side, c] * y_recv[sweep, side, c]
                    if last:
                        corr[c, plain_column(y), :] += scales[3] * more
                        if c == 0:
                            phase[padded_column(y), :] += scales[3] * more
                    else:
                        into[c, padded_column(y), :] += more

            receive(sweep, 3 - side, along_y)
        send(sweep + 1, (0, 1))
        for side in range(2):
            if last:
                y_send[sweep + 1, side, 0] = phase[padded_column(ends_y[side]), :]
            else:
                for c in range(2):
                    y_send[sweep + 1, side, c] = into[c, padded_column(ends_y[side]), :]
        send(sweep + 1, (2, 3))

    for sweep in range(SWEEPS):
        if sweep == SWEEPS - 1:
            load_pold.wait()
        def plane(x, sweep=sweep):
            for y in range(0, cy, 32):
                sweep_plane(sweep, x, y, 32)

        planes(0, cx, 4, plane)
        add_halos(sweep)

    wide = lax.broadcasted_iota(jnp.int32, (cy // 4, cz), 1)
    even = wide % 2 == 0
    half = cz // 2
    in_place = jnp.where(wide < half, 2 * wide, 2 * (wide - half) + 1)
    beside = jnp.where(wide < half, 2 * wide + 1, 2 * (wide - half))

    def pick(v, lanes):
        return jnp.take_along_axis(v, lanes, axis=1, mode="promise_in_bounds")

    def coarse_plane(part, i):
        sums = [None] * 2
        for x in (2 * i, 2 * i + 1):
            weight = 0.0625 * corr[1, plain(x), :]
            if part == 0:
                mid = phase[padded(x), :]
                before, after = along_depth(mid)
                fields = (0.125 * mid, weight * (after - before))
            else:
                fields = (
                    weight * (phase[padded(x + 1), :] - phase[padded(x - 1), :]),
                    weight * (phase[shifted(x, 1), :] - phase[shifted(x, -1), :]),
                )
            sums = [f if s is None else s + f for s, f in zip(sums, fields)]
        quarter = cy // 4
        slot = lax.rem(i, 4)
        for f in range(2):
            slab[slot, f] = sums[f]
        for f in range(2):
            rows = [slab[slot, f, pl.ds(k, quarter, stride=4), :] for k in range(4)]
            left, right = rows[0] + rows[1], rows[2] + rows[3]
            mean = pick(jnp.where(even, left, right), in_place)
            mean = mean + pick(jnp.where(even, right, left), beside)
            for q in range(4):
                packed[part, i * 4 + q, f * 4 : f * 4 + 4, :] = mean[q * 4 : q * 4 + 4, :]

    unit_rows = packed.shape[2]

    def unit_copy(part, peer):
        return pltpu.make_async_remote_copy(
            src_ref=stage.at[part, peer],
            dst_ref=recv.at[part, pl.ds(me * unit_rows, unit_rows)],
            send_sem=unit_send.at[part],
            recv_sem=unit_recv.at[part],
            device_id=peer,
            device_id_type=FLAT,
        )

    def ship(part):
        def one(k):
            peer = lax.rem(me + k, ndev)
            stage[part, peer] = packed[part, order[0, peer]]
            unit_copy(part, peer).start()

        planes(1, ndev - 1, 6, one)
        one(ndev - 1)
        recv[part, pl.ds(me * unit_rows, unit_rows), :] = packed[part, order[0, me]]

    def arrive(part):
        others = recv.at[part, pl.ds(0, (ndev - 1) * unit_rows)]
        pltpu.make_async_copy(others, others, unit_recv.at[part]).wait()

    save_order.wait()
    planes(0, cx // 2, 4, functools.partial(coarse_plane, 0))
    ship(0)
    for way in range(2):
        receive(SWEEPS, way, lambda: None)
    for side in range(2):

        def beyond(side=side):
            phase[padded_column((-1, cy)[side]), :] = y_recv[SWEEPS, side, 0]

        receive(SWEEPS, 3 - side, beyond)
    planes(0, cx // 2, 4, functools.partial(coarse_plane, 1))
    ship(1)

    for step in range(SWEEPS + 1):
        finish(step)
    load_vel.wait()

    product, get, factors = column_products(cz, recv)
    arrive(0)
    for r in range(4):
        at = pl.ds(r * cz, cz)
        parts = factors(r)
        for c in range(3):
            stress = product(vel[c, :, at], *parts)
            mom[c, :, at] = product(stress - get(0, 1, r), *parts) if c == 2 else stress
    arrive(1)

    for part in range(2):
        sent = stage.at[part, pl.ds(0, ndev - 1)]
        pltpu.make_async_copy(sent, sent, unit_send.at[part]).wait()


def output_body(cz, corr, mom, recv, corr_hbm, mom_hbm, rest, sem):
    size = corr.shape[1] * 2 // OUT_PIECES
    copies = []
    for i in range(OUT_PIECES):
        c, at = i % 2, pl.ds(i // 2 * size, size)
        copies.append(pltpu.make_async_copy(corr.at[c, at], corr_hbm.at[c, at], sem.at[i]))
    copies.append(pltpu.make_async_copy(mom.at[2], mom_hbm.at[2], sem.at[OUT_PIECES]))
    for copy in copies:
        copy.start()
    product, get, factors = column_products(cz, recv)
    for r in range(4):
        at = pl.ds(r * cz, cz)
        parts = factors(r)
        for c in range(2):
            rest[c, :, at] = product(mom[c, :, at] - get(1, c, r), *parts)
    store = pltpu.make_async_copy(rest, mom_hbm.at[pl.ds(0, 2)], sem.at[OUT_PIECES + 1])
    store.start()
    for copy in copies:
        copy.wait()
    store.wait()


def body(ngx, ngy, right_side, well_coef, mobility_coef, coupling, phase_old, unit_owner, velocity):
    _, cx, cy, cz = right_side.shape
    ndev = ngx * ngy
    chunks = 8
    unit_rows = 2 * (velocity.shape[2] // cz)
    flat = cx * cy
    padded = (cx + 2) * (cy + 2 * PAD)
    hbm_spec = pl.BlockSpec(memory_space=pltpu.HBM)
    vmem_spec = pl.BlockSpec(memory_space=pltpu.VMEM)
    f32 = jnp.float32
    steps = SWEEPS + 1
    hbm = lambda x: pltpu.with_memory_space_constraint(x, pltpu.HBM)
    parts = pl.pallas_call(
        functools.partial(kernel_body, (ngx, ngy, cx, cy, cz, chunks)),
        out_shape=(
            pltpu.VMEM((2, flat, cz), f32),
            pltpu.VMEM(velocity.shape, f32),
            pltpu.VMEM((2, ndev * unit_rows, cz), f32),
        ),
        in_specs=[hbm_spec] * 10,
        out_specs=(vmem_spec,) * 3,
        scratch_shapes=[
            pltpu.VMEM((1, ndev), jnp.int32),
            pltpu.VMEM((1, ndev), jnp.int32),
            pltpu.SMEM((1, ndev), jnp.int32),
            pltpu.VMEM((2, flat, cz), f32),
            pltpu.VMEM((2, 2, cx, cz), f32),
            pltpu.VMEM((2, 2, cx, cz), f32),
            pltpu.VMEM((flat, cz), f32),
            pltpu.VMEM((flat, cz), f32),
            pltpu.VMEM((2, padded, cz), f32),
            pltpu.VMEM((2, padded, cz), f32),
            pltpu.VMEM((2, padded, cz), f32),
            pltpu.VMEM((padded, cz), f32),
            pltpu.VMEM((SWEEPS, 2, 2, cy, cz), f32),
            pltpu.VMEM((steps, 2, 2, cx, cz), f32),
            pltpu.VMEM((steps, 2, 2, cx, cz), f32),
            pltpu.VMEM((4, 2, cy, cz), f32),
            pltpu.VMEM((2, ndev, unit_rows, cz), f32),
            pltpu.VMEM((2, ndev, unit_rows, cz), f32),
            pltpu.VMEM(velocity.shape, f32),
            pltpu.SemaphoreType.DMA((chunks, 3)),
            pltpu.SemaphoreType.DMA((2, 3)),
            pltpu.SemaphoreType.DMA((5,)),
            pltpu.SemaphoreType.DMA((steps, 4)),
            pltpu.SemaphoreType.DMA((steps, 4)),
            pltpu.SemaphoreType.DMA((2,)),
            pltpu.SemaphoreType.DMA((2,)),
        ],
        compiler_params=pltpu.CompilerParams(
            collective_id=0, has_side_effects=True, vmem_limit_bytes=48 * 1024 * 1024
        ),
    )(
        hbm(unit_owner.reshape(1, ndev)),
        hbm(right_side.reshape(2, flat, cz)),
        hbm(well_coef.reshape(flat, cz)),
        hbm(mobility_coef.reshape(flat, cz)),
        hbm(coupling.reshape(flat, cz)),
        hbm(phase_old.reshape(flat, cz)),
        hbm(velocity),
        hbm(right_side),
        hbm(well_coef),
        hbm(mobility_coef),
    )
    vmem = lambda x: pltpu.with_memory_space_constraint(x, pltpu.VMEM)
    correction, momentum = pl.pallas_call(
        functools.partial(output_body, cz),
        out_shape=(
            jax.ShapeDtypeStruct((2, flat, cz), f32),
            jax.ShapeDtypeStruct(velocity.shape, f32),
        ),
        in_specs=[vmem_spec] * 3,
        out_specs=(hbm_spec, hbm_spec),
        scratch_shapes=[
            pltpu.VMEM((2,) + velocity.shape[1:], f32),
            pltpu.SemaphoreType.DMA((OUT_PIECES + 2,)),
        ],
        compiler_params=pltpu.CompilerParams(vmem_limit_bytes=8 * 1024 * 1024),
    )(*[vmem(x) for x in parts])
    return correction.reshape(right_side.shape), momentum


def solution(mesh):
    return jax.shard_map(
        functools.partial(body, mesh.shape["gx"], mesh.shape["gy"]),
        mesh=mesh,
        in_specs=(
            P(None, "gx", "gy", None),
            P("gx", "gy", None),
            P("gx", "gy", None),
            P("gx", "gy", None),
            P("gx", "gy", None),
            P(("gx", "gy")),
            P(None, ("gx", "gy"), None),
        ),
        out_specs=(P(None, "gx", "gy", None), P(None, ("gx", "gy"), None)),
        check_vma=False,
    )
```

```python
import functools

import jax
import jax.numpy as jnp
from jax import lax
from jax.experimental import pallas as pl
from jax.experimental.pallas import tpu as pltpu
from jax.sharding import PartitionSpec as P

SWEEPS = 3
LOW_BOUND = 0.15
HIGH_BOUND = 1.85
THETA = (HIGH_BOUND + LOW_BOUND) / 2.0
DELTA = (HIGH_BOUND - LOW_BOUND) / 2.0
SIGMA = THETA / DELTA

PAD = 8
OUT_PIECES = 4
MESH = pl.DeviceIdType.MESH
FLAT = pl.DeviceIdType.LOGICAL


def recurrence():
    table, scales = [], [1.0]
    rho = 1.0 / SIGMA
    decay_before, gain_before = 0.0, 0.0
    for sweep in range(SWEEPS):
        rho_new = 1.0 / (2.0 * SIGMA - rho)
        decay, gain = rho_new * rho, 2.0 * rho_new / DELTA
        if sweep == 0:
            table.append(((decay + gain * (THETA - 1.0)) / gain, 0.0))
        else:
            ratio = gain / gain_before
            before = -ratio * decay_before * scales[-2] / (gain * scales[-1])
            table.append(((decay + ratio - gain) / gain, before))
        scales.append(scales[-1] * gain)
        decay_before, gain_before, rho = decay, gain, rho_new
    return table, scales


def column_products(cz, recv):
    unit_rows = 8
    units = recv.shape[1] // unit_rows
    lane = lax.broadcasted_iota(jnp.int32, (1, cz), 1)
    place = lax.rem(lane, cz // 2)
    bottom, top = place == 0, place == cz // 2 - 1

    def product(v, density, visc, weight):
        below = jnp.where(bottom, 0.0, pltpu.roll(v, 1, axis=1))
        flux = weight * (v - below)
        above = jnp.where(top, -visc * v, pltpu.roll(flux, cz - 1, axis=1))
        return density * v - (above - flux)

    def get(part, f, r):
        return recv[part, pl.ds(f * 4 + r, units, stride=unit_rows), :]

    def factors(r):
        mean = get(0, 0, r)
        density = 0.1 + 0.45 * (1.0 + mean)
        visc = 0.2 + 0.4 * (1.0 + mean)
        weight = 0.5 * (visc + jnp.where(bottom, visc, pltpu.roll(visc, 1, axis=1)))
        return density, visc, weight

    return product, get, factors


def kernel_body(
    sizes,
    owner,
    rhs_hbm,
    well_hbm,
    mob_hbm,
    cpl_hbm,
    pold_hbm,
    vel_hbm,
    rhs_rows,
    well_rows,
    mob_rows,
    corr,
    mom,
    recv,
    owner_row,
    order_row,
    order,
    inv,
    rhs_edge,
    inv_edge,
    cpl,
    pold,
    dir0,
    dir1,
    dir2,
    phase,
    x_recv,
    y_send,
    y_recv,
    slab,
    packed,
    stage,
    vel,
    load_sem,
    edge_sem,
    rest_sem,
    halo_send,
    halo_recv,
    unit_send,
    unit_recv,
):
    ngx, ngy, cx, cy, cz, chunks = sizes
    ndev = ngx * ngy
    gx, gy = lax.axis_index("gx"), lax.axis_index("gy")
    me = gx * ngy + gy
    per = cx // chunks
    pitch = cy + 2 * PAD
    f32 = jnp.float32

    def planes(first, last, together, work):
        def some(i, _):
            for k in range(together):
                work(first + i * together + k)
            return 0

        lax.fori_loop(0, (last - first) // together, some, 0)

    def padded(x, rows=cy):
        return pl.ds(pl.multiple_of((x + 1) * pitch + PAD, 8), rows)

    def shifted(x, by):
        return pl.ds((x + 1) * pitch + PAD + by, cy)

    def plain(x):
        return pl.ds(pl.multiple_of(x * cy, 8), cy)

    def padded_column(y):
        return pl.ds(pitch + PAD + y, cx, stride=pitch)

    def plain_column(y):
        return pl.ds(y, cx, stride=cy)

    ends_x, ends_y = (0, cx - 1), (0, cy - 1)

    barrier = pltpu.get_barrier_semaphore()

    def greet(k):
        pl.semaphore_signal(
            barrier, inc=1, device_id=lax.rem(me + k, ndev), device_id_type=FLAT
        )

    planes(1, ndev - 1, 21, greet)
    greet(ndev - 1)

    def load_chunk(i):
        at = pl.ds(i * per * cy, per * cy)
        return (
            pltpu.make_async_copy(rhs_hbm.at[:, at], corr.at[:, at], load_sem.at[i, 0]),
            pltpu.make_async_copy(well_hbm.at[at], inv.at[0, at], load_sem.at[i, 1]),
            pltpu.make_async_copy(mob_hbm.at[at], inv.at[1, at], load_sem.at[i, 2]),
        )

    def load_edge(side):
        y = ends_y[side]
        return (
            pltpu.make_async_copy(rhs_rows.at[:, :, y], rhs_edge.at[side], edge_sem.at[side, 0]),
            pltpu.make_async_copy(well_rows.at[:, y], inv_edge.at[side, 0], edge_sem.at[side, 1]),
            pltpu.make_async_copy(mob_rows.at[:, y], inv_edge.at[side, 1], edge_sem.at[side, 2]),
        )

    load_cpl = pltpu.make_async_copy(cpl_hbm, cpl, rest_sem.at[0])
    load_pold = pltpu.make_async_copy(pold_hbm, pold, rest_sem.at[1])
    load_vel = pltpu.make_async_copy(vel_hbm, vel, rest_sem.at[2])
    load_owner = pltpu.make_async_copy(owner, owner_row, rest_sem.at[4])
    load_owner.start()
    chunk_order = [0, chunks - 1] + list(range(1, chunks - 1))
    for side in range(2):
        for copy in load_edge(side):
            copy.start()
    for i in chunk_order:
        for copy in load_chunk(i):
            copy.start()
    load_cpl.start()
    load_pold.start()
    load_vel.start()

    down = lax.broadcasted_iota(jnp.int32, (ndev, ndev), 0)
    across = lax.broadcasted_iota(jnp.int32, (ndev, ndev), 1)
    load_owner.wait()
    unit_of = jnp.max(jnp.where(owner_row[...] == down, across, 0), axis=1, keepdims=True)
    order_row[...] = jnp.max(jnp.where(down == across, unit_of, 0), axis=0, keepdims=True)
    save_order = pltpu.make_async_copy(order_row, order, rest_sem.at[3])
    save_order.start()

    for buf in (dir0, dir1, dir2):
        for c in range(2):
            for x in (-1, cx):
                buf[c, padded(x), :] = jnp.zeros((cy, cz), f32)
            for y in (-1, cy):
                buf[c, padded_column(y), :] = jnp.zeros((cx, cz), f32)
    for y in (-1, cy):
        phase[padded_column(y), :] = jnp.zeros((cx, cz), f32)

    @pl.when(gx == 0)
    def _():
        phase[padded(-1), :] = jnp.zeros((cy, cz), f32)

    @pl.when(gx == ngx - 1)
    def _():
        phase[padded(cx), :] = jnp.zeros((cy, cz), f32)

    targets = ((gx - 1, gy), (gx + 1, gy), (gx, gy - 1), (gx, gy + 1))
    sends = (gx > 0, gx < ngx - 1, gy > 0, gy < ngy - 1)

    def halo_copy(step, way):
        side, other = way % 2, 1 - way % 2
        if way >= 2:
            src, dst = y_send.at[step, side], y_recv.at[step, other]
            if step == SWEEPS:
                src, dst = src.at[0], dst.at[0]
        elif step == SWEEPS:
            src, dst = phase.at[padded(ends_x[side])], phase.at[padded((-1, cx)[other])]
        else:
            src = (dir0, dir1, dir2)[step].at[:, padded(ends_x[side])]
            dst = x_recv.at[step, other]
        return pltpu.make_async_remote_copy(
            src_ref=src,
            dst_ref=dst,
            send_sem=halo_send.at[step, way],
            recv_sem=halo_recv.at[step, way],
            device_id=targets[way],
            device_id_type=MESH,
        )

    def send(step, ways):
        for way in ways:

            @pl.when(sends[way])
            def _(way=way):
                halo_copy(step, way).start()

    def receive(step, way, work):
        @pl.when(sends[way ^ 1])
        def _():
            halo_copy(step, way).wait_recv()
            work()

    def finish(step):
        for way in range(4):

            @pl.when(sends[way])
            def _(way=way):
                halo_copy(step, way).wait_send()

    lane = lax.broadcasted_iota(jnp.int32, (1, cz), 1)
    first_lane, last_lane = lane == 0, lane == cz - 1

    def along_depth(v):
        before = jnp.where(first_lane, 0.0, pltpu.roll(v, 1, axis=1))
        after = jnp.where(last_lane, 0.0, pltpu.roll(v, cz - 1, axis=1))
        return before, after

    def start_plane(x):
        for c in range(2):
            part = 1.0 / (inv[c, plain(x), :] + 6.0)
            inv[c, plain(x), :] = part
            dir0[c, padded(x), :] = part * corr[c, plain(x), :] * (1.0 / THETA)

    for side in range(2):
        for copy in load_edge(side):
            copy.wait()
        for c in range(2):
            part = 1.0 / (inv_edge[side, c] + 6.0)
            inv_edge[side, c] = part
            y_send[0, side, c] = part * rhs_edge[side, c] * (1.0 / THETA)
    for n, i in enumerate(chunk_order):
        for copy in load_chunk(i):
            copy.wait()
        planes(i * per, (i + 1) * per, 4, start_plane)
        if n == 1:
            pl.semaphore_wait(barrier, ndev - 1)
            send(0, (0, 1, 2, 3))
    load_cpl.wait()

    table, scales = recurrence()

    def own(x, y, rows):
        return pl.ds(pl.multiple_of((x + 1) * pitch + PAD + y, 8), rows)

    def sweep_plane(sweep, x, y, rows):
        now = (dir0, dir1, dir2)[sweep]
        of_now, of_before = table[sweep]
        mid = [now[c, own(x, y, rows), :] for c in range(2)]
        mix = cpl[pl.ds(pl.multiple_of(x * cy + y, 8), rows), :]
        for c in range(2):
            before, after = along_depth(mid[c])
            nbrs = now[c, own(x - 1, y, rows), :] + now[c, own(x + 1, y, rows), :]
            nbrs = nbrs + (now[c, pl.ds((x + 1) * pitch + PAD + y - 1, rows), :] + now[c, pl.ds((x + 1) * pitch + PAD + y + 1, rows), :])
            nbrs = nbrs + (before + after)
            new = of_now * mid[c] + inv[c, pl.ds(pl.multiple_of(x * cy + y, 8), rows), :] * (nbrs - mix * mid[1 - c])
            if sweep > 0:
                new = new + of_before * (dir0, dir1)[sweep - 1][c, own(x, y, rows), :]
            if sweep < SWEEPS - 1:
                (dir1, dir2)[sweep][c, own(x, y, rows), :] = new
            else:
                total = scales[0] * dir0[c, own(x, y, rows), :] + scales[1] * dir1[c, own(x, y, rows), :]
                total = total + (scales[2] * mid[c] + scales[3] * new)
                corr[c, pl.ds(pl.multiple_of(x * cy + y, 8), rows), :] = total
                if c == 0:
                    phase[own(x, y, rows), :] = pold[pl.ds(pl.multiple_of(x * cy + y, 8), rows), :] + total

    def add_halos(sweep):
        last = sweep == SWEEPS - 1
        into = None if last else (dir1, dir2)[sweep]
        for side in range(2):

            def along_x(side=side):
                x = ends_x[side]
                for c in range(2):
                    more = inv[c, plain(x), :] * x_recv[sweep, side, c]
                    if last:
                        corr[c, plain(x), :] += scales[3] * more
                        if c == 0:
                            phase[padded(x), :] += scales[3] * more
                    else:
                        into[c, padded(x), :] += more

            receive(sweep, 1 - side, along_x)
        for side in range(2):

            def along_y(side=side):
                y = ends_y[side]
                for c in range(2):
                    more = inv_edge[side, c] * y_recv[sweep, side, c]
                    if last:
                        corr[c, plain_column(y), :] += scales[3] * more
                        if c == 0:
                            phase[padded_column(y), :] += scales[3] * more
                    else:
                        into[c, padded_column(y), :] += more

            receive(sweep, 3 - side, along_y)
        send(sweep + 1, (0, 1))
        for side in range(2):
            if last:
                y_send[sweep + 1, side, 0] = phase[padded_column(ends_y[side]), :]
            else:
                for c in range(2):
                    y_send[sweep + 1, side, c] = into[c, padded_column(ends_y[side]), :]
        send(sweep + 1, (2, 3))

    wide = lax.broadcasted_iota(jnp.int32, (cy // 4, cz), 1)
    even = wide % 2 == 0
    half = cz // 2
    in_place = jnp.where(wide < half, 2 * wide, 2 * (wide - half) + 1)
    beside = jnp.where(wide < half, 2 * wide + 1, 2 * (wide - half))

    def pick(v, lanes):
        return jnp.take_along_axis(v, lanes, axis=1, mode="promise_in_bounds")

    def coarse_outer(i):
        sums = [None] * 2
        for x in (2 * i, 2 * i + 1):
            outer = lambda ref, at: jnp.concatenate(
                [ref[pl.ds(at, 8), :], ref[pl.ds(at + cy - 8, 8), :]], axis=0
            )
            mid = outer(phase, pl.multiple_of((x + 1) * pitch + PAD, 8))
            before, after = along_depth(mid)
            weight = 0.0625 * outer(corr.at[1], pl.multiple_of(x * cy, 8))
            fields = (0.125 * mid, weight * (after - before))
            sums = [f if s is None else s + f for s, f in zip(sums, fields)]
        slot = lax.rem(i, 4)
        for f in range(2):
            slab[slot, f, 0:16] = sums[f]
        for f in range(2):
            rows = [slab[slot, f, pl.ds(k, 4, stride=4), :] for k in range(4)]
            left, right = rows[0] + rows[1], rows[2] + rows[3]
            mean = pick(jnp.where(even[0:4], left, right), in_place[0:4])
            mean = mean + pick(jnp.where(even[0:4], right, left), beside[0:4])
            packed[0, i * 4, f * 4 : f * 4 + 2, :] = mean[0:2, :]
            packed[0, i * 4 + 3, f * 4 + 2 : f * 4 + 4, :] = mean[2:4, :]

    def coarse_plane(part, i):
        sums = [None] * 2
        for x in (2 * i, 2 * i + 1):
            weight = 0.0625 * corr[1, plain(x), :]
            if part == 0:
                mid = phase[padded(x), :]
                before, after = along_depth(mid)
                fields = (0.125 * mid, weight * (after - before))
            else:
                fields = (
                    weight * (phase[padded(x + 1), :] - phase[padded(x - 1), :]),
                    weight * (phase[shifted(x, 1), :] - phase[shifted(x, -1), :]),
                )
            sums = [f if s is None else s + f for s, f in zip(sums, fields)]
        quarter = cy // 4
        slot = lax.rem(i, 4)
        for f in range(2):
            slab[slot, f] = sums[f]
        for f in range(2):
            rows = [slab[slot, f, pl.ds(k, quarter, stride=4), :] for k in range(4)]
            left, right = rows[0] + rows[1], rows[2] + rows[3]
            mean = pick(jnp.where(even, left, right), in_place)
            mean = mean + pick(jnp.where(even, right, left), beside)
            for q in range(4):
                packed[part, i * 4 + q, f * 4 : f * 4 + 4, :] = mean[q * 4 : q * 4 + 4, :]

    for sweep in range(SWEEPS):
        if sweep == SWEEPS - 1:
            load_pold.wait()
        def plane(x, sweep=sweep):
            for y in range(0, cy, 32):
                sweep_plane(sweep, x, y, 32)

        planes(0, cx, 4, plane)
        if sweep == SWEEPS - 1:
            planes(0, cx // 2, 4, functools.partial(coarse_plane, 0))
        add_halos(sweep)

    unit_rows = packed.shape[2]

    def unit_copy(part, peer):
        return pltpu.make_async_remote_copy(
            src_ref=stage.at[part, peer],
            dst_ref=recv.at[part, pl.ds(me * unit_rows, unit_rows)],
            send_sem=unit_send.at[part],
            recv_sem=unit_recv.at[part],
            device_id=peer,
            device_id_type=FLAT,
        )

    def ship(part):
        def one(k):
            peer = lax.rem(me + k, ndev)
            stage[part, peer] = packed[part, order[0, peer]]
            unit_copy(part, peer).start()

        planes(1, ndev - 1, 14, one)
        one(ndev - 1)
        recv[part, pl.ds(me * unit_rows, unit_rows), :] = packed[part, order[0, me]]

    def arrive(part):
        others = recv.at[part, pl.ds(0, (ndev - 1) * unit_rows)]
        pltpu.make_async_copy(others, others, unit_recv.at[part]).wait()

    save_order.wait()
    coarse_plane(0, 0)
    coarse_plane(0, cx // 2 - 1)
    planes(1, cx // 2 - 1, 6, coarse_outer)
    ship(0)
    for way in range(2):
        receive(SWEEPS, way, lambda: None)
    for side in range(2):

        def beyond(side=side):
            phase[padded_column((-1, cy)[side]), :] = y_recv[SWEEPS, side, 0]

        receive(SWEEPS, 3 - side, beyond)
    planes(0, cx // 2, 4, functools.partial(coarse_plane, 1))
    ship(1)

    for step in range(SWEEPS + 1):
        finish(step)
    load_vel.wait()

    product, get, factors = column_products(cz, recv)
    arrive(0)
    for r in range(4):
        at = pl.ds(r * cz, cz)
        parts = factors(r)
        for c in range(3):
            stress = product(vel[c, :, at], *parts)
            mom[c, :, at] = product(stress - get(0, 1, r), *parts) if c == 2 else stress
    arrive(1)

    for part in range(2):
        sent = stage.at[part, pl.ds(0, ndev - 1)]
        pltpu.make_async_copy(sent, sent, unit_send.at[part]).wait()


def output_body(cz, corr, mom, recv, corr_hbm, mom_hbm, rest, sem):
    size = corr.shape[1] * 2 // OUT_PIECES
    copies = []
    for i in range(OUT_PIECES):
        c, at = i % 2, pl.ds(i // 2 * size, size)
        copies.append(pltpu.make_async_copy(corr.at[c, at], corr_hbm.at[c, at], sem.at[i]))
    copies.append(pltpu.make_async_copy(mom.at[2], mom_hbm.at[2], sem.at[OUT_PIECES]))
    for copy in copies:
        copy.start()
    product, get, factors = column_products(cz, recv)
    for r in range(4):
        at = pl.ds(r * cz, cz)
        parts = factors(r)
        for c in range(2):
            rest[c, :, at] = product(mom[c, :, at] - get(1, c, r), *parts)
    store = pltpu.make_async_copy(rest, mom_hbm.at[pl.ds(0, 2)], sem.at[OUT_PIECES + 1])
    store.start()
    for copy in copies:
        copy.wait()
    store.wait()


def body(ngx, ngy, right_side, well_coef, mobility_coef, coupling, phase_old, unit_owner, velocity):
    _, cx, cy, cz = right_side.shape
    ndev = ngx * ngy
    chunks = 8
    unit_rows = 2 * (velocity.shape[2] // cz)
    flat = cx * cy
    padded = (cx + 2) * (cy + 2 * PAD)
    hbm_spec = pl.BlockSpec(memory_space=pltpu.HBM)
    vmem_spec = pl.BlockSpec(memory_space=pltpu.VMEM)
    f32 = jnp.float32
    steps = SWEEPS + 1
    hbm = lambda x: pltpu.with_memory_space_constraint(x, pltpu.HBM)
    parts = pl.pallas_call(
        functools.partial(kernel_body, (ngx, ngy, cx, cy, cz, chunks)),
        out_shape=(
            pltpu.VMEM((2, flat, cz), f32),
            pltpu.VMEM(velocity.shape, f32),
            pltpu.VMEM((2, ndev * unit_rows, cz), f32),
        ),
        in_specs=[hbm_spec] * 10,
        out_specs=(vmem_spec,) * 3,
        scratch_shapes=[
            pltpu.VMEM((1, ndev), jnp.int32),
            pltpu.VMEM((1, ndev), jnp.int32),
            pltpu.SMEM((1, ndev), jnp.int32),
            pltpu.VMEM((2, flat, cz), f32),
            pltpu.VMEM((2, 2, cx, cz), f32),
            pltpu.VMEM((2, 2, cx, cz), f32),
            pltpu.VMEM((flat, cz), f32),
            pltpu.VMEM((flat, cz), f32),
            pltpu.VMEM((2, padded, cz), f32),
            pltpu.VMEM((2, padded, cz), f32),
            pltpu.VMEM((2, padded, cz), f32),
            pltpu.VMEM((padded, cz), f32),
            pltpu.VMEM((SWEEPS, 2, 2, cy, cz), f32),
            pltpu.VMEM((steps, 2, 2, cx, cz), f32),
            pltpu.VMEM((steps, 2, 2, cx, cz), f32),
            pltpu.VMEM((4, 2, cy, cz), f32),
            pltpu.VMEM((2, ndev, unit_rows, cz), f32),
            pltpu.VMEM((2, ndev, unit_rows, cz), f32),
            pltpu.VMEM(velocity.shape, f32),
            pltpu.SemaphoreType.DMA((chunks, 3)),
            pltpu.SemaphoreType.DMA((2, 3)),
            pltpu.SemaphoreType.DMA((5,)),
            pltpu.SemaphoreType.DMA((steps, 4)),
            pltpu.SemaphoreType.DMA((steps, 4)),
            pltpu.SemaphoreType.DMA((2,)),
            pltpu.SemaphoreType.DMA((2,)),
        ],
        compiler_params=pltpu.CompilerParams(
            collective_id=0, has_side_effects=True, vmem_limit_bytes=48 * 1024 * 1024
        ),
    )(
        hbm(unit_owner.reshape(1, ndev)),
        hbm(right_side.reshape(2, flat, cz)),
        hbm(well_coef.reshape(flat, cz)),
        hbm(mobility_coef.reshape(flat, cz)),
        hbm(coupling.reshape(flat, cz)),
        hbm(phase_old.reshape(flat, cz)),
        hbm(velocity),
        hbm(right_side),
        hbm(well_coef),
        hbm(mobility_coef),
    )
    vmem = lambda x: pltpu.with_memory_space_constraint(x, pltpu.VMEM)
    correction, momentum = pl.pallas_call(
        functools.partial(output_body, cz),
        out_shape=(
            jax.ShapeDtypeStruct((2, flat, cz), f32),
            jax.ShapeDtypeStruct(velocity.shape, f32),
        ),
        in_specs=[vmem_spec] * 3,
        out_specs=(hbm_spec, hbm_spec),
        scratch_shapes=[
            pltpu.VMEM((2,) + velocity.shape[1:], f32),
            pltpu.SemaphoreType.DMA((OUT_PIECES + 2,)),
        ],
        compiler_params=pltpu.CompilerParams(vmem_limit_bytes=8 * 1024 * 1024),
    )(*[vmem(x) for x in parts])
    return correction.reshape(right_side.shape), momentum


def solution(mesh):
    return jax.shard_map(
        functools.partial(body, mesh.shape["gx"], mesh.shape["gy"]),
        mesh=mesh,
        in_specs=(
            P(None, "gx", "gy", None),
            P("gx", "gy", None),
            P("gx", "gy", None),
            P("gx", "gy", None),
            P("gx", "gy", None),
            P(("gx", "gy")),
            P(None, ("gx", "gy"), None),
        ),
        out_specs=(P(None, "gx", "gy", None), P(None, ("gx", "gy"), None)),
        check_vma=False,
    )
```

```python
import functools

import jax
import jax.numpy as jnp
from jax import lax
from jax.experimental import pallas as pl
from jax.experimental.pallas import tpu as pltpu
from jax.sharding import PartitionSpec as P

SWEEPS = 3
LOW_BOUND = 0.15
HIGH_BOUND = 1.85
THETA = (HIGH_BOUND + LOW_BOUND) / 2.0
DELTA = (HIGH_BOUND - LOW_BOUND) / 2.0
SIGMA = THETA / DELTA

PAD = 8
OUT_PIECES = 4
MESH = pl.DeviceIdType.MESH
FLAT = pl.DeviceIdType.LOGICAL


def recurrence():
    table, scales = [], [1.0]
    rho = 1.0 / SIGMA
    decay_before, gain_before = 0.0, 0.0
    for sweep in range(SWEEPS):
        rho_new = 1.0 / (2.0 * SIGMA - rho)
        decay, gain = rho_new * rho, 2.0 * rho_new / DELTA
        if sweep == 0:
            table.append(((decay + gain * (THETA - 1.0)) / gain, 0.0))
        else:
            ratio = gain / gain_before
            before = -ratio * decay_before * scales[-2] / (gain * scales[-1])
            table.append(((decay + ratio - gain) / gain, before))
        scales.append(scales[-1] * gain)
        decay_before, gain_before, rho = decay, gain, rho_new
    return table, scales


def column_products(cz, recv):
    unit_rows = 8
    units = recv.shape[1] // unit_rows
    lane = lax.broadcasted_iota(jnp.int32, (1, cz), 1)
    place = lax.rem(lane, cz // 2)
    bottom, top = place == 0, place == cz // 2 - 1

    def product(v, density, visc, weight):
        below = jnp.where(bottom, 0.0, pltpu.roll(v, 1, axis=1))
        flux = weight * (v - below)
        above = jnp.where(top, -visc * v, pltpu.roll(flux, cz - 1, axis=1))
        return density * v - (above - flux)

    def get(part, f, r):
        return recv[part, pl.ds(f * 4 + r, units, stride=unit_rows), :]

    def factors(r):
        mean = get(0, 0, r)
        density = 0.1 + 0.45 * (1.0 + mean)
        visc = 0.2 + 0.4 * (1.0 + mean)
        weight = 0.5 * (visc + jnp.where(bottom, visc, pltpu.roll(visc, 1, axis=1)))
        return density, visc, weight

    return product, get, factors


def kernel_body(
    sizes,
    owner,
    rhs_hbm,
    well_hbm,
    mob_hbm,
    cpl_hbm,
    pold_hbm,
    vel_hbm,
    rhs_rows,
    well_rows,
    mob_rows,
    corr,
    mom,
    recv,
    owner_row,
    order_row,
    order,
    inv,
    rhs_edge,
    inv_edge,
    cpl,
    pold,
    dir0,
    dir1,
    dir2,
    phase,
    x_recv,
    y_send,
    y_recv,
    slab,
    packed,
    stage,
    vel,
    load_sem,
    edge_sem,
    rest_sem,
    halo_send,
    halo_recv,
    unit_send,
    unit_recv,
):
    ngx, ngy, cx, cy, cz, chunks = sizes
    ndev = ngx * ngy
    gx, gy = lax.axis_index("gx"), lax.axis_index("gy")
    me = gx * ngy + gy
    per = cx // chunks
    pitch = cy + 2 * PAD
    f32 = jnp.float32

    def planes(first, last, together, work):
        def some(i, _):
            for k in range(together):
                work(first + i * together + k)
            return 0

        lax.fori_loop(0, (last - first) // together, some, 0)

    def padded(x, rows=cy):
        return pl.ds(pl.multiple_of((x + 1) * pitch + PAD, 8), rows)

    def shifted(x, by):
        return pl.ds((x + 1) * pitch + PAD + by, cy)

    def plain(x):
        return pl.ds(pl.multiple_of(x * cy, 8), cy)

    def padded_column(y):
        return pl.ds(pitch + PAD + y, cx, stride=pitch)

    def plain_column(y):
        return pl.ds(y, cx, stride=cy)

    ends_x, ends_y = (0, cx - 1), (0, cy - 1)

    barrier = pltpu.get_barrier_semaphore()

    def greet(k):
        pl.semaphore_signal(
            barrier, inc=1, device_id=lax.rem(me + k, ndev), device_id_type=FLAT
        )

    planes(1, ndev - 1, 9, greet)
    greet(ndev - 1)

    def load_chunk(i):
        at = pl.ds(i * per * cy, per * cy)
        return (
            pltpu.make_async_copy(rhs_hbm.at[:, at], corr.at[:, at], load_sem.at[i, 0]),
            pltpu.make_async_copy(well_hbm.at[at], inv.at[0, at], load_sem.at[i, 1]),
            pltpu.make_async_copy(mob_hbm.at[at], inv.at[1, at], load_sem.at[i, 2]),
        )

    def load_edge(side):
        y = ends_y[side]
        return (
            pltpu.make_async_copy(rhs_rows.at[:, :, y], rhs_edge.at[side], edge_sem.at[side, 0]),
            pltpu.make_async_copy(well_rows.at[:, y], inv_edge.at[side, 0], edge_sem.at[side, 1]),
            pltpu.make_async_copy(mob_rows.at[:, y], inv_edge.at[side, 1], edge_sem.at[side, 2]),
        )

    load_cpl = pltpu.make_async_copy(cpl_hbm, cpl, rest_sem.at[0])
    load_pold = pltpu.make_async_copy(pold_hbm, pold, rest_sem.at[1])
    load_vel = pltpu.make_async_copy(vel_hbm, vel, rest_sem.at[2])
    load_owner = pltpu.make_async_copy(owner, owner_row, rest_sem.at[4])
    load_owner.start()
    chunk_order = [0, chunks - 1] + list(range(1, chunks - 1))
    for side in range(2):
        for copy in load_edge(side):
            copy.start()
    for i in chunk_order:
        for copy in load_chunk(i):
            copy.start()
    load_cpl.start()
    load_pold.start()
    load_vel.start()

    down = lax.broadcasted_iota(jnp.int32, (ndev, ndev), 0)
    across = lax.broadcasted_iota(jnp.int32, (ndev, ndev), 1)
    load_owner.wait()
    unit_of = jnp.max(jnp.where(owner_row[...] == down, across, 0), axis=1, keepdims=True)
    order_row[...] = jnp.max(jnp.where(down == across, unit_of, 0), axis=0, keepdims=True)
    save_order = pltpu.make_async_copy(order_row, order, rest_sem.at[3])
    save_order.start()

    for buf in (dir0, dir1, dir2):
        for c in range(2):
            for x in (-1, cx):
                buf[c, padded(x), :] = jnp.zeros((cy, cz), f32)
            for y in (-1, cy):
                buf[c, padded_column(y), :] = jnp.zeros((cx, cz), f32)
    for y in (-1, cy):
        phase[padded_column(y), :] = jnp.zeros((cx, cz), f32)

    @pl.when(gx == 0)
    def _():
        phase[padded(-1), :] = jnp.zeros((cy, cz), f32)

    @pl.when(gx == ngx - 1)
    def _():
        phase[padded(cx), :] = jnp.zeros((cy, cz), f32)

    targets = ((gx - 1, gy), (gx + 1, gy), (gx, gy - 1), (gx, gy + 1))
    sends = (gx > 0, gx < ngx - 1, gy > 0, gy < ngy - 1)

    def halo_copy(step, way):
        side, other = way % 2, 1 - way % 2
        if way >= 2:
            src, dst = y_send.at[step, side], y_recv.at[step, other]
            if step == SWEEPS:
                src, dst = src.at[0], dst.at[0]
        elif step == SWEEPS:
            src, dst = phase.at[padded(ends_x[side])], phase.at[padded((-1, cx)[other])]
        else:
            src = (dir0, dir1, dir2)[step].at[:, padded(ends_x[side])]
            dst = x_recv.at[step, other]
        return pltpu.make_async_remote_copy(
            src_ref=src,
            dst_ref=dst,
            send_sem=halo_send.at[step, way],
            recv_sem=halo_recv.at[step, way],
            device_id=targets[way],
            device_id_type=MESH,
        )

    def send(step, ways):
        for way in ways:

            @pl.when(sends[way])
            def _(way=way):
                halo_copy(step, way).start()

    def receive(step, way, work):
        @pl.when(sends[way ^ 1])
        def _():
            halo_copy(step, way).wait_recv()
            work()

    def finish(step):
        for way in range(4):

            @pl.when(sends[way])
            def _(way=way):
                halo_copy(step, way).wait_send()

    lane = lax.broadcasted_iota(jnp.int32, (1, cz), 1)
    first_lane, last_lane = lane == 0, lane == cz - 1

    def along_depth(v):
        before = jnp.where(first_lane, 0.0, pltpu.roll(v, 1, axis=1))
        after = jnp.where(last_lane, 0.0, pltpu.roll(v, cz - 1, axis=1))
        return before, after

    def start_plane(x):
        for c in range(2):
            part = 1.0 / (inv[c, plain(x), :] + 6.0)
            inv[c, plain(x), :] = part
            dir0[c, padded(x), :] = part * corr[c, plain(x), :] * (1.0 / THETA)

    for side in range(2):
        for copy in load_edge(side):
            copy.wait()
        for c in range(2):
            part = 1.0 / (inv_edge[side, c] + 6.0)
            inv_edge[side, c] = part
            y_send[0, side, c] = part * rhs_edge[side, c] * (1.0 / THETA)
    for n, i in enumerate(chunk_order):
        for copy in load_chunk(i):
            copy.wait()
        planes(i * per, (i + 1) * per, 4, start_plane)
        if n == 1:
            pl.semaphore_wait(barrier, ndev - 1)
            send(0, (0, 1, 2, 3))
    load_cpl.wait()

    table, scales = recurrence()

    def own(x, y, rows):
        return pl.ds(pl.multiple_of((x + 1) * pitch + PAD + y, 8), rows)

    def sweep_plane(sweep, x, y, rows):
        now = (dir0, dir1, dir2)[sweep]
        of_now, of_before = table[sweep]
        mid = [now[c, own(x, y, rows), :] for c in range(2)]
        mix = cpl[pl.ds(pl.multiple_of(x * cy + y, 8), rows), :]
        for c in range(2):
            before, after = along_depth(mid[c])
            nbrs = now[c, own(x - 1, y, rows), :] + now[c, own(x + 1, y, rows), :]
            nbrs = nbrs + (now[c, pl.ds((x + 1) * pitch + PAD + y - 1, rows), :] + now[c, pl.ds((x + 1) * pitch + PAD + y + 1, rows), :])
            nbrs = nbrs + (before + after)
            new = of_now * mid[c] + inv[c, pl.ds(pl.multiple_of(x * cy + y, 8), rows), :] * (nbrs - mix * mid[1 - c])
            if sweep > 0:
                new = new + of_before * (dir0, dir1)[sweep - 1][c, own(x, y, rows), :]
            if sweep < SWEEPS - 1:
                (dir1, dir2)[sweep][c, own(x, y, rows), :] = new
            else:
                total = scales[0] * dir0[c, own(x, y, rows), :] + scales[1] * dir1[c, own(x, y, rows), :]
                total = total + (scales[2] * mid[c] + scales[3] * new)
                corr[c, pl.ds(pl.multiple_of(x * cy + y, 8), rows), :] = total
                if c == 0:
                    phase[own(x, y, rows), :] = pold[pl.ds(pl.multiple_of(x * cy + y, 8), rows), :] + total

    def add_halos(sweep):
        last = sweep == SWEEPS - 1
        into = None if last else (dir1, dir2)[sweep]
        for side in range(2):

            def along_x(side=side):
                x = ends_x[side]
                for c in range(2):
                    more = inv[c, plain(x), :] * x_recv[sweep, side, c]
                    if last:
                        if c == 0:
                            phase[padded(x), :] += scales[3] * more
                    else:
                        into[c, padded(x), :] += more

            receive(sweep, 1 - side, along_x)
        for side in range(2):

            def along_y(side=side):
                y = ends_y[side]
                for c in range(2):
                    more = inv_edge[side, c] * y_recv[sweep, side, c]
                    if last:
                        if c == 0:
                            phase[padded_column(y), :] += scales[3] * more
                    else:
                        into[c, padded_column(y), :] += more

            receive(sweep, 3 - side, along_y)
        send(sweep + 1, (0, 1))
        for side in range(2):
            if last:
                y_send[sweep + 1, side, 0] = phase[padded_column(ends_y[side]), :]
            else:
                for c in range(2):
                    y_send[sweep + 1, side, c] = into[c, padded_column(ends_y[side]), :]
        send(sweep + 1, (2, 3))
        for side in range(2) if last else ():

            @pl.when(sends[side])
            def _(side=side):
                at = plain(ends_x[side])
                for c in range(2):
                    corr[c, at, :] += scales[3] * (inv[c, at, :] * x_recv[sweep, side, c])

        for side in range(2) if last else ():

            @pl.when(sends[2 + side])
            def _(side=side):
                at = plain_column(ends_y[side])
                for c in range(2):
                    corr[c, at, :] += scales[3] * (inv_edge[side, c] * y_recv[sweep, side, c])

    for sweep in range(SWEEPS):
        if sweep == SWEEPS - 1:
            load_pold.wait()
        def plane(x, sweep=sweep):
            for y in range(0, cy, 32):
                sweep_plane(sweep, x, y, 32)

        planes(0, cx, 4, plane)
        add_halos(sweep)

    wide = lax.broadcasted_iota(jnp.int32, (cy // 4, cz), 1)
    even = wide % 2 == 0
    half = cz // 2
    in_place = jnp.where(wide < half, 2 * wide, 2 * (wide - half) + 1)
    beside = jnp.where(wide < half, 2 * wide + 1, 2 * (wide - half))

    def pick(v, lanes):
        return jnp.take_along_axis(v, lanes, axis=1, mode="promise_in_bounds")

    def coarse_plane(part, i):
        sums = [None] * 2
        for x in (2 * i, 2 * i + 1):
            weight = 0.0625 * corr[1, plain(x), :]
            if part == 0:
                mid = phase[padded(x), :]
                before, after = along_depth(mid)
                fields = (0.125 * mid, weight * (after - before))
            else:
                fields = (
                    weight * (phase[padded(x + 1), :] - phase[padded(x - 1), :]),
                    weight * (phase[shifted(x, 1), :] - phase[shifted(x, -1), :]),
                )
            sums = [f if s is None else s + f for s, f in zip(sums, fields)]
        quarter = cy // 4
        slot = lax.rem(i, 4)
        for f in range(2):
            slab[slot, f] = sums[f]
        for f in range(2):
            rows = [slab[slot, f, pl.ds(k, quarter, stride=4), :] for k in range(4)]
            left, right = rows[0] + rows[1], rows[2] + rows[3]
            mean = pick(jnp.where(even, left, right), in_place)
            mean = mean + pick(jnp.where(even, right, left), beside)
            for q in range(4):
                packed[part, i * 4 + q, f * 4 : f * 4 + 4, :] = mean[q * 4 : q * 4 + 4, :]

    unit_rows = packed.shape[2]

    def unit_copy(part, peer):
        return pltpu.make_async_remote_copy(
            src_ref=stage.at[part, peer],
            dst_ref=recv.at[part, pl.ds(me * unit_rows, unit_rows)],
            send_sem=unit_send.at[part],
            recv_sem=unit_recv.at[part],
            device_id=peer,
            device_id_type=FLAT,
        )

    def ship(part):
        def one(k):
            peer = lax.rem(me + k, ndev)
            stage[part, peer] = packed[part, order[0, peer]]
            unit_copy(part, peer).start()

        planes(1, ndev - 1, 6, one)
        one(ndev - 1)
        recv[part, pl.ds(me * unit_rows, unit_rows), :] = packed[part, order[0, me]]

    def arrive(part):
        others = recv.at[part, pl.ds(0, (ndev - 1) * unit_rows)]
        pltpu.make_async_copy(others, others, unit_recv.at[part]).wait()

    save_order.wait()
    planes(0, cx // 2, 4, functools.partial(coarse_plane, 0))
    ship(0)
    for way in range(2):
        receive(SWEEPS, way, lambda: None)
    for side in range(2):

        def beyond(side=side):
            phase[padded_column((-1, cy)[side]), :] = y_recv[SWEEPS, side, 0]

        receive(SWEEPS, 3 - side, beyond)
    planes(0, cx // 2, 4, functools.partial(coarse_plane, 1))
    ship(1)

    for step in range(SWEEPS + 1):
        finish(step)
    load_vel.wait()

    product, get, factors = column_products(cz, recv)
    arrive(0)
    for r in range(4):
        at = pl.ds(r * cz, cz)
        parts = factors(r)
        for c in range(3):
            stress = product(vel[c, :, at], *parts)
            mom[c, :, at] = product(stress - get(0, 1, r), *parts) if c == 2 else stress
    arrive(1)

    for part in range(2):
        sent = stage.at[part, pl.ds(0, ndev - 1)]
        pltpu.make_async_copy(sent, sent, unit_send.at[part]).wait()


def output_body(cz, corr, mom, recv, corr_hbm, mom_hbm, rest, sem):
    size = corr.shape[1] * 2 // OUT_PIECES
    copies = []
    for i in range(OUT_PIECES):
        c, at = i % 2, pl.ds(i // 2 * size, size)
        copies.append(pltpu.make_async_copy(corr.at[c, at], corr_hbm.at[c, at], sem.at[i]))
    copies.append(pltpu.make_async_copy(mom.at[2], mom_hbm.at[2], sem.at[OUT_PIECES]))
    for copy in copies:
        copy.start()
    product, get, factors = column_products(cz, recv)
    for r in range(4):
        at = pl.ds(r * cz, cz)
        parts = factors(r)
        for c in range(2):
            rest[c, :, at] = product(mom[c, :, at] - get(1, c, r), *parts)
    store = pltpu.make_async_copy(rest, mom_hbm.at[pl.ds(0, 2)], sem.at[OUT_PIECES + 1])
    store.start()
    for copy in copies:
        copy.wait()
    store.wait()


def body(ngx, ngy, right_side, well_coef, mobility_coef, coupling, phase_old, unit_owner, velocity):
    _, cx, cy, cz = right_side.shape
    ndev = ngx * ngy
    chunks = 8
    unit_rows = 2 * (velocity.shape[2] // cz)
    flat = cx * cy
    padded = (cx + 2) * (cy + 2 * PAD)
    hbm_spec = pl.BlockSpec(memory_space=pltpu.HBM)
    vmem_spec = pl.BlockSpec(memory_space=pltpu.VMEM)
    f32 = jnp.float32
    steps = SWEEPS + 1
    hbm = lambda x: pltpu.with_memory_space_constraint(x, pltpu.HBM)
    parts = pl.pallas_call(
        functools.partial(kernel_body, (ngx, ngy, cx, cy, cz, chunks)),
        out_shape=(
            pltpu.VMEM((2, flat, cz), f32),
            pltpu.VMEM(velocity.shape, f32),
            pltpu.VMEM((2, ndev * unit_rows, cz), f32),
        ),
        in_specs=[hbm_spec] * 10,
        out_specs=(vmem_spec,) * 3,
        scratch_shapes=[
            pltpu.VMEM((1, ndev), jnp.int32),
            pltpu.VMEM((1, ndev), jnp.int32),
            pltpu.SMEM((1, ndev), jnp.int32),
            pltpu.VMEM((2, flat, cz), f32),
            pltpu.VMEM((2, 2, cx, cz), f32),
            pltpu.VMEM((2, 2, cx, cz), f32),
            pltpu.VMEM((flat, cz), f32),
            pltpu.VMEM((flat, cz), f32),
            pltpu.VMEM((2, padded, cz), f32),
            pltpu.VMEM((2, padded, cz), f32),
            pltpu.VMEM((2, padded, cz), f32),
            pltpu.VMEM((padded, cz), f32),
            pltpu.VMEM((SWEEPS, 2, 2, cy, cz), f32),
            pltpu.VMEM((steps, 2, 2, cx, cz), f32),
            pltpu.VMEM((steps, 2, 2, cx, cz), f32),
            pltpu.VMEM((4, 2, cy, cz), f32),
            pltpu.VMEM((2, ndev, unit_rows, cz), f32),
            pltpu.VMEM((2, ndev, unit_rows, cz), f32),
            pltpu.VMEM(velocity.shape, f32),
            pltpu.SemaphoreType.DMA((chunks, 3)),
            pltpu.SemaphoreType.DMA((2, 3)),
            pltpu.SemaphoreType.DMA((5,)),
            pltpu.SemaphoreType.DMA((steps, 4)),
            pltpu.SemaphoreType.DMA((steps, 4)),
            pltpu.SemaphoreType.DMA((2,)),
            pltpu.SemaphoreType.DMA((2,)),
        ],
        compiler_params=pltpu.CompilerParams(
            collective_id=0, has_side_effects=True, vmem_limit_bytes=48 * 1024 * 1024
        ),
    )(
        hbm(unit_owner.reshape(1, ndev)),
        hbm(right_side.reshape(2, flat, cz)),
        hbm(well_coef.reshape(flat, cz)),
        hbm(mobility_coef.reshape(flat, cz)),
        hbm(coupling.reshape(flat, cz)),
        hbm(phase_old.reshape(flat, cz)),
        hbm(velocity),
        hbm(right_side),
        hbm(well_coef),
        hbm(mobility_coef),
    )
    vmem = lambda x: pltpu.with_memory_space_constraint(x, pltpu.VMEM)
    correction, momentum = pl.pallas_call(
        functools.partial(output_body, cz),
        out_shape=(
            jax.ShapeDtypeStruct((2, flat, cz), f32),
            jax.ShapeDtypeStruct(velocity.shape, f32),
        ),
        in_specs=[vmem_spec] * 3,
        out_specs=(hbm_spec, hbm_spec),
        scratch_shapes=[
            pltpu.VMEM((2,) + velocity.shape[1:], f32),
            pltpu.SemaphoreType.DMA((OUT_PIECES + 2,)),
        ],
        compiler_params=pltpu.CompilerParams(vmem_limit_bytes=8 * 1024 * 1024),
    )(*[vmem(x) for x in parts])
    return correction.reshape(right_side.shape), momentum


def solution(mesh):
    return jax.shard_map(
        functools.partial(body, mesh.shape["gx"], mesh.shape["gy"]),
        mesh=mesh,
        in_specs=(
            P(None, "gx", "gy", None),
            P("gx", "gy", None),
            P("gx", "gy", None),
            P("gx", "gy", None),
            P("gx", "gy", None),
            P(("gx", "gy")),
            P(None, ("gx", "gy"), None),
        ),
        out_specs=(P(None, "gx", "gy", None), P(None, ("gx", "gy"), None)),
        check_vma=False,
    )
```
